32 devices in a mesh: batch: 8 (over z, x), seq: 4 (over y, core).
Axes of the slice: x: 2, y: 2, z: 4, core: 2. Of those that a mesh axis runs over, the one named last changes fastest.
Arguments:
- tokens: bfloat16 [16384, 768], P(('batch', 'seq')), may hold values from -6 to 6
- cotangent: bfloat16 [16384, 768], P(('batch', 'seq')), may hold values from -6 to 6
- cond: bfloat16 [32, 128], P('batch'), may hold values from -6 to 6
- seq_lengths: int32 [32], P('batch'), may hold values from 0 to 2048, as said below
- adaptive_master: float32 [128, 4608], P(None, ('batch', 'seq')), may hold values from -0.5 to 0.5
- attention_master: float32 [768, 3072], P(None, ('batch', 'seq'))
- feedforward_master: float32 [2, 768, 3072], P(None, None, ('batch', 'seq')), may hold values from -0.21875 to 0.21875
- vector_master: float32 [9984], P(('batch', 'seq'))
- adaptive_first: float32 [128, 4608], P(None, ('batch', 'seq')), may hold values from -48 to 48
- attention_first: float32 [768, 3072], P(None, ('batch', 'seq')), may hold values from -32 to 32
- feedforward_first: float32 [2, 768, 3072], P(None, None, ('batch', 'seq')), may hold values from -32 to 32
- vector_first: float32 [9984], P(('batch', 'seq')), may hold values from -48 to 48
- adaptive_second: float32 [128, 4608], P(None, ('batch', 'seq')), may hold values from 5.89824 to 23.59296
- attention_second: float32 [768, 3072], P(None, ('batch', 'seq')), may hold values from 1.96608 to 8.02816
- feedforward_second: float32 [2, 768, 3072], P(None, None, ('batch', 'seq')), may hold values from 2.62144 to 10.48576
- vector_second: float32 [9984], P(('batch', 'seq')), may hold values from 5.89824 to 23.59296
Outputs:
- block_output: bfloat16 [16384, 768], P(('batch', 'seq'))
- input_grad: bfloat16 [16384, 768], P(('batch', 'seq'))
- adaptive_updated: float32 [128, 4608], P(None, ('batch', 'seq'))
- adaptive_first_new: float32 [128, 4608], P(None, ('batch', 'seq'))
- adaptive_second_new: float32 [128, 4608], P(None, ('batch', 'seq'))
- adaptive_copy: bfloat16 [128, 4608], P(None, ('batch', 'seq'))
- attention_updated: float32 [768, 3072], P(None, ('batch', 'seq'))
- attention_first_new: float32 [768, 3072], P(None, ('batch', 'seq'))
- attention_second_new: float32 [768, 3072], P(None, ('batch', 'seq'))
- attention_copy: bfloat16 [768, 3072], P(None, ('batch', 'seq'))
- feedforward_updated: float32 [2, 768, 3072], P(None, None, ('batch', 'seq'))
- feedforward_first_new: float32 [2, 768, 3072], P(None, None, ('batch', 'seq'))
- feedforward_second_new: float32 [2, 768, 3072], P(None, None, ('batch', 'seq'))
- feedforward_copy: bfloat16 [2, 768, 3072], P(None, None, ('batch', 'seq'))
- vector_updated: float32 [9984], P(('batch', 'seq'))
- vector_first_new: float32 [9984], P(('batch', 'seq'))
- vector_second_new: float32 [9984], P(('batch', 'seq'))
- vector_copy: bfloat16 [9984], P(('batch', 'seq'))
The draws below stay inside these ranges and needn't reach their ends.
Inputs may be any that keep to these rules, and one draw needn't show every extreme that they name: `seq_lengths`: the 4 lengths of each group are either 2048 followed by zeros (one sequence) or 512 each; at least one group holds one sequence.
All inputs are finite; a program needn't handle non-finite values.
Results may differ from the reference program's by a relative error of at most 0.018.
The reference program's roundings to bfloat16 on the way count: a program that leaves them out, or rounds other values in their place, can miss the bound.
Values may be sent and summed in bfloat16 or wider, within the bound.
No kernel may reach another device: no remote copies, remote signals or barrier semaphores. Data moves between devices by JAX's collectives and lax.ppermute only.
A program may use at most 192 MiB of HBM per device.

```python
import math
import jax
import jax.numpy as jnp
from jax import lax

D = 768
HEADS = 12
HEAD_DIM = 64
FF = 3072
COND = 128
SLOTS = 4
STEP = 10
GROUP_TOK = 2048
SHORT_LEN = 512
GROUPS = 8
TOKENS = 16384
SMALL = 9984


def draw_attention_master(key, part):
    key_in = jax.random.fold_in(key, 11)
    key_out = jax.random.fold_in(key, 12)
    inner_part = 0.045 * jax.random.normal(key_in, (D, 3 * D), jnp.float32)
    outer_part = 0.09 * jax.random.normal(key_out, (D, D), jnp.float32)
    return jnp.concatenate([inner_part, outer_part], axis=1)


def draw_vector_master(key, part):
    gain_one = 1.0 + 0.1 * jax.random.uniform(jax.random.fold_in(key, 21), (D,), jnp.float32, -2.5, 2.5)
    gain_two = 1.0 + 0.1 * jax.random.uniform(jax.random.fold_in(key, 22), (D,), jnp.float32, -2.5, 2.5)
    bias_up = 0.2 * jax.random.normal(jax.random.fold_in(key, 23), (FF,), jnp.float32)
    bias_down = 0.2 * jax.random.normal(jax.random.fold_in(key, 24), (D,), jnp.float32)
    bias_mod = 0.3 * jax.random.normal(jax.random.fold_in(key, 25), (6 * D,), jnp.float32)
    return jnp.concatenate([gain_one, gain_two, bias_up, bias_down, bias_mod])


def draw_seq_lengths(key, part):
    long_flags = jax.random.randint(jax.random.fold_in(key, 31), (GROUPS,), 0, 3) == 0
    forced = jax.random.randint(jax.random.fold_in(key, 32), (), 0, GROUPS)
    single = long_flags | (jnp.arange(GROUPS) == forced)
    long_row = jnp.where(jnp.arange(SLOTS) == 0, GROUP_TOK, 0)
    short_row = jnp.full((SLOTS,), SHORT_LEN)
    length_table = jnp.where(single[:, None], long_row[None, :], short_row[None, :])
    return length_table.reshape(GROUPS * SLOTS).astype(jnp.int32)


def level_of(rng, extent, cuts, least, top_value):
    factor_of = 1.0
    for position, shards_of in cuts:
        steps = jax.random.uniform(jax.random.fold_in(jax.random.fold_in(rng, 6), position), (shards_of,), jnp.float32, least / len(cuts), top_value / len(cuts))
        factor_of = factor_of * jnp.repeat(jnp.exp(steps), extent[position] // shards_of).reshape((-1,) + (1,) * (len(extent) - 1 - position))
    return factor_of


def normal_values(own_key, extent, deviation, bound, shards=(), kind=jnp.bfloat16):
    drawn = jax.random.normal(own_key, extent, jnp.float32) * deviation
    if len(shards) > 0:
        drawn = level_of(own_key, extent, shards, -0.22, 0.18) * drawn
    return jnp.clip(drawn, min=-bound, max=bound).astype(kind)


def setup_inputs(seed: int = 0) -> dict:
    keys = jax.random.split(jax.random.key(seed), 17)
    return {
        "tokens": normal_values(keys[0], (TOKENS, D), 1.0, 6.0, ((0, 32),)),
        "cotangent": normal_values(keys[1], (TOKENS, D), 1.0, 6.0, ((0, 32),)),
        "cond": normal_values(keys[2], (GROUPS * SLOTS, COND), 1.0, 6.0, ((0, 8),)),
        "seq_lengths": draw_seq_lengths(jax.random.fold_in(keys[16], 71), 0),
        "adaptive_master": normal_values(keys[4], (COND, 6 * D), COND ** -0.5, 0.5, ((1, 32),), jnp.float32),
        "attention_master": draw_attention_master(jax.random.fold_in(keys[16], 71), 0),
        "feedforward_master": normal_values(keys[6], (2, D, FF), D ** -0.5, 0.21875, ((2, 32),), jnp.float32),
        "vector_master": draw_vector_master(jax.random.fold_in(keys[16], 71), 0),
        "adaptive_first": normal_values(keys[8], (COND, 6 * D), (0.067 * TOKENS ** 0.5), 48.0, ((1, 32),), jnp.float32),
        "attention_first": normal_values(keys[9], (D, 4 * D), (0.039 * TOKENS ** 0.5), 32.0, ((1, 32),), jnp.float32),
        "feedforward_first": normal_values(keys[10], (2, D, FF), (0.044 * TOKENS ** 0.5), 32.0, ((2, 32),), jnp.float32),
        "vector_first": normal_values(keys[11], (SMALL,), (0.067 * TOKENS ** 0.5), 48.0, ((0, 32),), jnp.float32),
        "adaptive_second": jnp.clip(jnp.exp(math.log(23.59296) - 1.3862944 * jax.random.uniform(keys[12], (COND, 6 * D), jnp.float32) ** level_of(keys[12], (COND, 6 * D), ((1, 32),), -0.2, 0.2)), 5.89824, 23.59296),
        "attention_second": jnp.clip(jnp.exp(math.log(8.02816) - 1.40691369 * jax.random.uniform(keys[13], (D, 4 * D), jnp.float32) ** level_of(keys[13], (D, 4 * D), ((1, 32),), -0.2, 0.2)), 1.96608, 8.02816),
        "feedforward_second": jnp.clip(jnp.exp(math.log(10.48576) - 1.3862944 * jax.random.uniform(keys[14], (2, D, FF), jnp.float32) ** level_of(keys[14], (2, D, FF), ((2, 32),), -0.2, 0.2)), 2.62144, 10.48576),
        "vector_second": jnp.clip(jnp.exp(math.log(23.59296) - 1.3862944 * jax.random.uniform(keys[15], (SMALL,), jnp.float32) ** level_of(keys[15], (SMALL,), ((0, 32),), -0.2, 0.2)), 5.89824, 23.59296),
    }


@jax.custom_vjp
def low(v):
    return lax.optimization_barrier(v.astype(jnp.bfloat16)).astype(jnp.float32)

@jax.custom_vjp
def low_back(v):
    return v

def low_keep(v):
    return (low(v), None)

def low_pass(kept, grad):
    return (grad,)

def back_keep(v):
    return (v, None)

def back_low(kept, grad):
    return (low(grad),)
low.defvjp(low_keep, low_pass)
low_back.defvjp(back_keep, back_low)
beta_one = 0.9
beta_two = 0.999
adam_eps = 1e-08
decay_rate = 0.1
norm_eps = 1e-06
rate_adaptive = 0.15
rate_attention = 0.08
rate_forward = 0.07
rate_vector = 0.4
highest = lax.Precision.HIGHEST

def modnorm(values, gain, shift, scale):
    centre = values - lax.optimization_barrier(jnp.mean(values, axis=-1, keepdims=True))
    spread = lax.optimization_barrier(jnp.mean(centre * centre, axis=-1, keepdims=True))
    normed = centre * lax.rsqrt(spread + norm_eps)
    return normed * gain * (1.0 + scale) + shift

def rotate(values, places):
    half_dim = values.shape[-1] // 2
    freqs = 10000.0 ** (-jnp.arange(half_dim, dtype=jnp.float32) * 2.0 / values.shape[-1])
    angles = places.astype(jnp.float32)[:, None] * freqs[None, :]
    cosine = jnp.concatenate([jnp.cos(angles), jnp.cos(angles)], axis=-1)[:, None, :]
    sine = jnp.concatenate([jnp.sin(angles), jnp.sin(angles)], axis=-1)[:, None, :]
    turned = jnp.concatenate([-values[..., half_dim:], values[..., :half_dim]], axis=-1)
    return values * cosine + turned * sine

def seq_layout(lengths, places):
    ends = jnp.cumsum(lengths).astype(jnp.int32)
    starts = ends - lengths
    seq_index = lax.optimization_barrier(jnp.sum((places[:, None] >= ends[None, :]).astype(jnp.int32), axis=1)).astype(jnp.int32)
    picker = seq_index[:, None] == jnp.arange(lengths.shape[0], dtype=jnp.int32)[None, :]
    offsets = places - lax.optimization_barrier(jnp.sum(jnp.where(picker, starts[None, :], 0), axis=1)).astype(jnp.int32)
    return (seq_index, offsets, picker)

def attention(query_all, key_all, value_all, seq_ids):
    block_rows = min(512, GROUP_TOK)
    blocks = GROUP_TOK // block_rows

    def one_block(blk):
        start = (blk * block_rows).astype(jnp.int32)
        q_block = lax.dynamic_slice_in_dim(query_all, start, block_rows, 0)
        q_ids = lax.dynamic_slice_in_dim(seq_ids, start, block_rows, 0)
        raw = low_back(jnp.einsum('qhd,khd->hqk', q_block, key_all, precision=highest) * 0.125)
        masked = jnp.where(q_ids[None, :, None] == seq_ids[None, None, :], raw, -1e+30)
        top = lax.optimization_barrier(jnp.max(masked, axis=-1, keepdims=True))
        expo = jnp.exp(masked - top)
        probs = low(expo / lax.optimization_barrier(jnp.sum(expo, axis=-1, keepdims=True)))
        return jnp.einsum('hqk,khd->qhd', probs, value_all, precision=highest)
    outs = lax.map(jax.checkpoint(one_block), jnp.arange(blocks, dtype=jnp.int32))
    return outs.reshape(GROUP_TOK, HEADS, HEAD_DIM)

def group_block(inputs_g, cond_g, lengths_g, adaptive_w, attention_w, forward_w, vector_w):
    gain_one = vector_w[:D]
    gain_two = vector_w[D:2 * D]
    bias_up = vector_w[2 * D:2 * D + FF]
    bias_down = vector_w[2 * D + FF:3 * D + FF]
    bias_mod = vector_w[3 * D + FF:]
    silu_low = low(jax.nn.silu(cond_g))
    mod_slots = jnp.dot(silu_low, adaptive_w, precision=highest) + bias_mod
    places = jnp.arange(GROUP_TOK, dtype=jnp.int32)
    seq_ids, offsets, picker = seq_layout(lengths_g, places)
    mod_tokens = mod_slots[seq_ids]
    shift_one = mod_tokens[:, 0:D]
    scale_one = mod_tokens[:, D:2 * D]
    gate_one = mod_tokens[:, 2 * D:3 * D]
    shift_two = mod_tokens[:, 3 * D:4 * D]
    scale_two = mod_tokens[:, 4 * D:5 * D]
    gate_two = mod_tokens[:, 5 * D:6 * D]
    normed_one = low(modnorm(inputs_g, gain_one, shift_one, scale_one))
    qkv_vals = low_back(jnp.dot(normed_one, attention_w[:, :3 * D], precision=highest))
    query_rot = rotate(qkv_vals[:, :D].reshape(GROUP_TOK, HEADS, HEAD_DIM), offsets)
    key_rot = rotate(qkv_vals[:, D:2 * D].reshape(GROUP_TOK, HEADS, HEAD_DIM), offsets)
    value_vals = qkv_vals[:, 2 * D:].reshape(GROUP_TOK, HEADS, HEAD_DIM)
    query_low = low(low_back(query_rot))
    key_low = low(low_back(key_rot))
    value_low = low(low_back(value_vals))
    attended = attention(query_low, key_low, value_low, seq_ids).reshape(GROUP_TOK, D)
    attended = low(low_back(attended))
    attn_out = low_back(jnp.dot(attended, attention_w[:, 3 * D:], precision=highest))
    middle = inputs_g + gate_one * attn_out
    normed_two = low(modnorm(middle, gain_two, shift_two, scale_two))
    up_vals = low_back(jnp.dot(normed_two, forward_w[0], precision=highest) + bias_up)
    act_vals = low(jax.nn.gelu(up_vals, approximate=True))
    ffn_out = low_back(jnp.einsum('tf,df->td', act_vals, forward_w[1], precision=highest) + bias_down)
    return middle + gate_two * ffn_out

def adamw_update(master, first, second, grad, rate):
    first_new = beta_one * first + (1.0 - beta_one) * grad
    second_new = beta_two * second + (1.0 - beta_two) * grad * grad
    first_hat = first_new / (1.0 - beta_one ** STEP)
    second_hat = second_new / (1.0 - beta_two ** STEP)
    master_new = master - rate * (first_hat / (jnp.sqrt(second_hat) + adam_eps) + decay_rate * master)
    return (master_new, first_new, second_new, master_new.astype(jnp.bfloat16))

def reference(tokens, cotangent, cond, seq_lengths, adaptive_master, attention_master, feedforward_master, vector_master, adaptive_first, attention_first, feedforward_first, vector_first, adaptive_second, attention_second, feedforward_second, vector_second):
    groups = TOKENS // GROUP_TOK
    adaptive_c = adaptive_master.astype(jnp.bfloat16).astype(jnp.float32)
    attention_c = attention_master.astype(jnp.bfloat16).astype(jnp.float32)
    forward_c = feedforward_master.astype(jnp.bfloat16).astype(jnp.float32)
    vector_c = vector_master.astype(jnp.bfloat16).astype(jnp.float32)
    inputs_f = tokens.astype(jnp.float32).reshape(groups, GROUP_TOK, D)
    cond_f = cond.astype(jnp.float32).reshape(groups, SLOTS, COND)
    length_rows = seq_lengths.reshape(groups, SLOTS)

    def forward(inputs_all, adaptive_w, attention_w, forward_w, vector_w):

        def one_group(packed_in):
            return group_block(packed_in[0], packed_in[1], packed_in[2], adaptive_w, attention_w, forward_w, vector_w)
        return lax.map(jax.checkpoint(one_group), (inputs_all, cond_f, length_rows))
    outputs, pullback = jax.vjp(forward, inputs_f, adaptive_c, attention_c, forward_c, vector_c)
    grads = pullback(cotangent.astype(jnp.float32).reshape(groups, GROUP_TOK, D))
    block_output = outputs.reshape(TOKENS, D).astype(jnp.bfloat16)
    input_grad = grads[0].reshape(TOKENS, D).astype(jnp.bfloat16)
    adaptive_res = adamw_update(adaptive_master, adaptive_first, adaptive_second, grads[1], rate_adaptive)
    attention_res = adamw_update(attention_master, attention_first, attention_second, grads[2], rate_attention)
    forward_res = adamw_update(feedforward_master, feedforward_first, feedforward_second, grads[3], rate_forward)
    vector_res = adamw_update(vector_master, vector_first, vector_second, grads[4], rate_vector)
    return (block_output, input_grad, adaptive_res[0], adaptive_res[1], adaptive_res[2], adaptive_res[3], attention_res[0], attention_res[1], attention_res[2], attention_res[3], forward_res[0], forward_res[1], forward_res[2], forward_res[3], vector_res[0], vector_res[1], vector_res[2], vector_res[3])
```

```python
import math
from functools import partial

import jax
import jax.numpy as jnp
from jax import lax
from jax.experimental import pallas as pl
from jax.experimental.pallas import tpu as pltpu
from jax.sharding import PartitionSpec as P

D = 768
HEADS = 12
HEAD_DIM = 64
HALF = 32
FF = 3072
COND = 128
SLOTS = 4
STEP = 10
ALL = ("batch", "seq")

beta_one = 0.9
beta_two = 0.999
adam_eps = 1e-08
decay_rate = 0.1
norm_eps = 1e-06
rate_adaptive = 0.15
rate_attention = 0.08
rate_forward = 0.07
rate_vector = 0.4
bf16 = jnp.bfloat16
f32 = jnp.float32
EXPO = math.log2(math.e) * 0.125


def mm(a, b, ca, cb):
    return lax.dot_general(a, b, (((ca,), (cb,)), ((), ())), preferred_element_type=f32)


def swap(v, stage):
    axis, bit = stage
    size = lax.axis_size(axis)
    return lax.ppermute(v, axis, [(i, i ^ bit) for i in range(size)])


def gather_rel(v, stages):
    for stage in stages:
        v = jnp.concatenate([v, swap(v, stage)], axis=0)
    return v


def scatter_rel(v, stages):
    for stage in reversed(stages):
        half = v.shape[0] // 2
        got = swap(v[half:], stage)
        v = (v[:half].astype(f32) + got.astype(f32)).astype(bf16)
    return v


def masks_of(stages, seq_size):
    out = [0]
    for axis, bit in stages:
        whole = bit * seq_size if axis == "batch" else bit
        out = out + [m | whole for m in out]
    return out


def places_of(stages, seq_size, count):
    masks = masks_of(stages, seq_size)
    where = [0] * count
    for k, m in enumerate(masks):
        where[m] = k
    return where


def bits_down(size):
    return [1 << i for i in reversed(range(size.bit_length() - 1))]


def adamw_update(master, first, second, grad, rate):
    first_new = beta_one * first + (1.0 - beta_one) * grad
    second_new = beta_two * second + (1.0 - beta_two) * grad * grad
    first_hat = first_new / (1.0 - beta_one**STEP)
    second_hat = second_new / (1.0 - beta_two**STEP)
    master_new = master - rate * (
        first_hat / (jnp.sqrt(second_hat) + adam_eps) + decay_rate * master
    )
    return (master_new, first_new, second_new, master_new.astype(bf16))


def rope(v, cos, sin):
    v1, v2 = v[:HALF], v[HALF:]
    return jnp.concatenate([v1 * cos - v2 * sin, v2 * cos + v1 * sin], axis=0)


def rope_back(v, cos, sin):
    v1, v2 = v[:HALF], v[HALF:]
    return jnp.concatenate([v1 * cos + v2 * sin, v2 * cos - v1 * sin], axis=0)


def qkv_kernel(pa, pb, x_ref, gain_ref, shift_ref, wa_ref, wb_ref, cos_ref, sin_ref, h_ref, q_ref, w_ref):
    part = wa_ref.shape[1]
    chunks = w_ref.shape[0] // (2 * part)

    @pl.when(pl.program_id(0) == 0)
    def _():
        for k in range(chunks):
            w_ref[2 * part * k : 2 * part * k + part, :] = wa_ref[pa[k]]
            w_ref[2 * part * k + part : 2 * part * (k + 1), :] = wb_ref[pb[k]]

    x = x_ref[0].astype(f32)
    mean = jnp.mean(x, axis=-1, keepdims=True)
    centre = x - mean
    var = jnp.mean(centre * centre, axis=-1, keepdims=True)
    h = centre * lax.rsqrt(var + norm_eps) * gain_ref[0] + shift_ref[0]
    h = h.astype(bf16)
    h_ref[0] = h
    out = mm(w_ref[...], h, 1, 1)
    cos, sin = cos_ref[0], sin_ref[0]
    rows = out.shape[0] // 3
    for i in range(2 * rows // HEAD_DIM):
        at = i * HEAD_DIM
        q_ref[0, at : at + HEAD_DIM, :] = rope(out[at : at + HEAD_DIM], cos, sin).astype(bf16)
    q_ref[0, 2 * rows :, :] = out[2 * rows :].astype(bf16)


def split_two(v):
    hi = v.astype(bf16)
    return hi, (v - hi.astype(f32)).astype(bf16)


def three_rows(v, rows):
    a = v.astype(bf16).astype(f32)
    b = (v - a).astype(bf16).astype(f32)
    c = v - a - b
    at = lax.broadcasted_iota(jnp.int32, (rows, v.shape[1]), 0)
    out = jnp.where(at == 0, a, jnp.where(at == 1, b, jnp.where(at == 2, c, 0.0)))
    return out.astype(bf16)


def forward_kernel(long_ref, q_ref, k_ref, v_ref, o_ref, of_ref, l_ref, kk):
    blocks, _, rows = k_ref.shape
    qb = pl.program_id(1)

    @pl.when(qb == 0)
    def _():
        for r in range(blocks):
            k = k_ref[r]
            kk[r * rows : (r + 1) * rows, :] = jnp.concatenate([k, k], axis=0).T

    hi, lo = split_two(q_ref[0].astype(f32) * EXPO)
    query = jnp.concatenate([hi, lo], axis=0)

    def finish(out, total, top):
        out = out / total
        of_ref[0] = out
        o_ref[0] = out.astype(bf16)
        l_ref[0, 0] = top + jnp.log2(total)

    @pl.when(long_ref[0] == 1)
    def _():
        scores = [mm(kk[r * rows : (r + 1) * rows, :], query, 1, 0) for r in range(blocks)]
        top = jnp.max(scores[0], axis=0, keepdims=True)
        for s in scores[1:]:
            top = jnp.maximum(top, jnp.max(s, axis=0, keepdims=True))
        out = jnp.zeros((HEAD_DIM, rows), f32)
        total = jnp.zeros((1, rows), f32)
        for r in range(blocks):
            e = jnp.exp2(scores[r] - top)
            total = total + jnp.sum(e, axis=0, keepdims=True)
            out = out + mm(v_ref[r], e.astype(bf16), 1, 0)
        finish(out, total, top)

    @pl.when(long_ref[0] == 0)
    def _():
        start = pl.multiple_of(qb * rows, rows)
        s = mm(kk[pl.ds(start, rows), :], query, 1, 0)
        top = jnp.max(s, axis=0, keepdims=True)
        e = jnp.exp2(s - top)
        total = jnp.sum(e, axis=0, keepdims=True)
        finish(mm(v_ref[qb], e.astype(bf16), 1, 0), total, top)


def backward_kernel(
    long_ref, q_ref, k_ref, v_ref, do_ref, of_ref, l_ref, cos_ref, sin_ref,
    dq_ref, dk_ref, dv_ref, kk, vv, dk, dv,
):
    blocks, _, rows = k_ref.shape
    qb = pl.program_id(1)

    @pl.when(qb == 0)
    def _():
        for r in range(blocks):
            k, v = k_ref[r], v_ref[r]
            one = jnp.ones((HEAD_DIM, rows), bf16)
            span = slice(r * rows, (r + 1) * rows)
            kk[span, :] = jnp.concatenate([k, k, one, one], axis=0).T
            vv[span, :] = jnp.concatenate([v, one], axis=0).T
        dk[...] = jnp.zeros_like(dk)
        dv[...] = jnp.zeros_like(dv)

    q = q_ref[0]
    do = do_ref[0]
    hi, lo = split_two(q.astype(f32) * EXPO)
    query = jnp.concatenate([hi, lo, three_rows(-l_ref[0, 0], 2 * HEAD_DIM)], axis=0)
    delta = jnp.sum(do.astype(f32) * of_ref[0], axis=0, keepdims=True)
    grad = jnp.concatenate([do, three_rows(-delta, HEAD_DIM)], axis=0)
    q_rows = q.T
    do_rows = do.T
    cos, sin = cos_ref[qb], sin_ref[qb]

    def one(start, k):
        span = pl.ds(start, rows)
        p = jnp.exp2(mm(kk[span, :], query, 1, 0))
        ds = (p * mm(vv[span, :], grad, 1, 0)).astype(bf16)
        dv[span, :] += mm(p.astype(bf16), do_rows, 1, 0)
        dk[span, :] += mm(ds, q_rows, 1, 0)
        return mm(k, ds, 1, 0)

    def finish(total):
        dq_ref[0] = rope_back(total * 0.125, cos, sin).astype(bf16)

    @pl.when(long_ref[0] == 1)
    def _():
        total = one(0, k_ref[0])
        for r in range(1, blocks):
            total = total + one(r * rows, k_ref[r])
        finish(total)

    @pl.when(long_ref[0] == 0)
    def _():
        finish(one(pl.multiple_of(qb * rows, rows), k_ref[qb]))

    @pl.when(qb == blocks - 1)
    def _():
        for r in range(blocks):
            span = slice(r * rows, (r + 1) * rows)
            dk_ref[r] = rope_back(dk[span, :].T * 0.125, cos_ref[r], sin_ref[r]).astype(bf16)
            dv_ref[r] = dv[span, :].T.astype(bf16)


def qkv_back_kernel(dq_ref, dk_ref, dv_ref, h_ref, w_ref, dh_ref, dw_ref, acc):
    b = pl.program_id(0)
    g = jnp.concatenate([dq_ref[0], dk_ref[0], dv_ref[0]], axis=0)
    dw = mm(g, h_ref[0], 1, 0)

    @pl.when(b == 0)
    def _():
        acc[...] = dw

    @pl.when(b > 0)
    def _():
        acc[...] += dw

    @pl.when(b == pl.num_programs(0) - 1)
    def _():
        dw_ref[...] = acc[...].astype(bf16)

    dh_ref[0] = mm(g.T, w_ref[...], 1, 0).astype(bf16)


def full(shape):
    return pl.BlockSpec(shape, lambda *_: (0,) * len(shape))


SMEM = pl.BlockSpec(memory_space=pltpu.SMEM)
ONE = pltpu.CompilerParams(dimension_semantics=("arbitrary",))
TWO = pltpu.CompilerParams(dimension_semantics=("arbitrary", "arbitrary"))


def qkv_call(pa, pb, x, gain, shift, wa, wb, cos, sin):
    blocks, rows, _ = x.shape
    feats = 3 * wa.shape[0] * (wa.shape[1] + wb.shape[1]) // 4
    block = lambda *s: pl.BlockSpec((1,) + s, lambda b: (b, 0, 0))
    return pl.pallas_call(
        qkv_kernel,
        name="qkv",
        grid=(blocks,),
        in_specs=[SMEM, SMEM, block(rows, D), block(1, D), block(1, D), full(wa.shape), full(wb.shape), block(HALF, rows), block(HALF, rows)],
        out_specs=[block(rows, D), block(feats, rows), full((feats, D))],
        out_shape=[
            jax.ShapeDtypeStruct((blocks, rows, D), bf16),
            jax.ShapeDtypeStruct((blocks, feats, rows), bf16),
            jax.ShapeDtypeStruct((feats, D), bf16),
        ],
        compiler_params=ONE,
    )(pa, pb, x, gain, shift, wa, wb, cos, sin)


def forward_call(long, qkv, heads):
    blocks, _, rows = qkv.shape
    part = lambda n: pl.BlockSpec((blocks, HEAD_DIM, rows), lambda h, b, n=n: (0, n * heads + h, 0))
    own = pl.BlockSpec((1, HEAD_DIM, rows), lambda h, b: (b, h, 0))
    feats = heads * HEAD_DIM
    return pl.pallas_call(
        forward_kernel,
        name="attn_fwd",
        grid=(heads, blocks),
        in_specs=[SMEM, own, part(1), part(2)],
        out_specs=[own, own, pl.BlockSpec((1, 1, 1, rows), lambda h, b: (h, b, 0, 0))],
        out_shape=[
            jax.ShapeDtypeStruct((blocks, feats, rows), bf16),
            jax.ShapeDtypeStruct((blocks, feats, rows), f32),
            jax.ShapeDtypeStruct((heads, blocks, 1, rows), f32),
        ],
        scratch_shapes=[pltpu.VMEM((blocks * rows, 2 * HEAD_DIM), bf16)],
        compiler_params=TWO,
    )(long, qkv, qkv, qkv)


def backward_call(long, qkv, do, of, lse, cos, sin, heads):
    blocks, _, rows = qkv.shape
    part = lambda n: pl.BlockSpec((blocks, HEAD_DIM, rows), lambda h, b, n=n: (0, n * heads + h, 0))
    own = pl.BlockSpec((1, HEAD_DIM, rows), lambda h, b: (b, h, 0))
    feats = heads * HEAD_DIM
    shape = jax.ShapeDtypeStruct((blocks, feats, rows), bf16)
    return pl.pallas_call(
        backward_kernel,
        name="attn_bwd",
        grid=(heads, blocks),
        in_specs=[SMEM, own, part(1), part(2), own, own, pl.BlockSpec((1, 1, 1, rows), lambda h, b: (h, b, 0, 0)), full(cos.shape), full(sin.shape)],
        out_specs=[own, part(0), part(0)],
        out_shape=[shape, shape, shape],
        scratch_shapes=[
            pltpu.VMEM((blocks * rows, 4 * HEAD_DIM), bf16),
            pltpu.VMEM((blocks * rows, 2 * HEAD_DIM), bf16),
            pltpu.VMEM((blocks * rows, HEAD_DIM), f32),
            pltpu.VMEM((blocks * rows, HEAD_DIM), f32),
        ],
        compiler_params=TWO,
    )(long, qkv, qkv, qkv, do, of, lse, cos, sin)


def qkv_back_call(dq, dk, dv, h, w):
    blocks, feats, rows = dq.shape
    block = lambda *s: pl.BlockSpec((1,) + s, lambda b: (b, 0, 0))
    return pl.pallas_call(
        qkv_back_kernel,
        name="qkv_bwd",
        grid=(blocks,),
        in_specs=[block(feats, rows)] * 3 + [block(rows, D), full(w.shape)],
        out_specs=[block(rows, D), full(w.shape)],
        out_shape=[
            jax.ShapeDtypeStruct((blocks, rows, D), bf16),
            jax.ShapeDtypeStruct(w.shape, bf16),
        ],
        scratch_shapes=[pltpu.VMEM(w.shape, f32)],
        compiler_params=ONE,
    )(dq, dk, dv, h, w)


def on_device(
    tokens, cotangent, cond, seq_lengths,
    adaptive_master, attention_master, feedforward_master, vector_master,
    adaptive_first, attention_first, feedforward_first, vector_first,
    adaptive_second, attention_second, feedforward_second, vector_second,
):
    rows = tokens.shape[0]
    seq_size = lax.axis_size("seq")
    batch_size = lax.axis_size("batch")
    world = seq_size * batch_size
    heads = HEADS // seq_size
    seat = lax.axis_index("seq")
    place = lax.axis_index("batch")
    me = place * seq_size + seat
    seq_stages = [("seq", b) for b in bits_down(seq_size)]
    batch_bits = bits_down(batch_size)
    far_first = [("batch", b) for b in batch_bits]
    near_first = [("batch", batch_bits[-1])] + [("batch", b) for b in batch_bits[:-1]]
    seq_masks = masks_of(seq_stages, seq_size)
    chunk = attention_master.shape[1]
    half = chunk // 2

    cs = jax.nn.silu(cond.astype(f32)).astype(bf16)
    split = (seq_lengths[1] > 0).astype(jnp.int32)
    vec_part = vector_master.shape[0]
    vec_rows = -(-vec_part // COND)
    vec_pad = jnp.pad(vector_master.astype(bf16), (0, vec_rows * COND - vec_part))
    flag = jnp.full((1, COND), 1.0, bf16) * split.astype(bf16)
    small = jnp.concatenate([cs, flag, vec_pad.reshape(vec_rows, COND)], axis=0)
    small = jnp.broadcast_to(small[None], (world,) + small.shape)
    small_all = lax.all_to_all(small, ALL, 0, 0, tiled=True)
    cs_all = small_all[::seq_size, :SLOTS].reshape(batch_size * SLOTS, COND)
    split_all = small_all[::seq_size, SLOTS, 0] > 0
    vector_f = small_all[:, SLOTS + 1 :].reshape(world, vec_rows * COND)[:, :vec_part]
    vector_f = vector_f.reshape(-1).astype(f32)
    gain_one = vector_f[:D]
    gain_two = vector_f[D : 2 * D]
    bias_up = vector_f[2 * D : 2 * D + FF]
    bias_down = vector_f[2 * D + FF : 3 * D + FF]
    bias_mod = vector_f[3 * D + FF :]
    mod_part = adaptive_master.shape[1]
    mod_cols = mm(cs_all, adaptive_master.astype(bf16), 1, 0)
    mod_send = jnp.broadcast_to(
        mod_cols.reshape(batch_size, 1, SLOTS, mod_part), (batch_size, seq_size, SLOTS, mod_part)
    ).reshape(world, SLOTS, mod_part)
    mod_got = lax.all_to_all(mod_send, ALL, 0, 0, tiled=True)
    mod = jnp.swapaxes(mod_got, 0, 1).reshape(SLOTS, world * mod_part) + bias_mod

    x_all = gather_rel(tokens[None], seq_stages)
    slot_of = [split * (seat ^ m) for m in seq_masks]
    mod_here = [lax.dynamic_index_in_dim(mod, s, 0, keepdims=True) for s in slot_of]
    gain_rows = jnp.stack([gain_one * (1.0 + m[:, D : 2 * D]) for m in mod_here])
    shift_rows = jnp.stack([m[:, :D] for m in mod_here])
    own_mod = mod_here[0]
    scale_one = own_mod[:, D : 2 * D]
    gate_one = own_mod[:, 2 * D : 3 * D]
    shift_two = own_mod[:, 3 * D : 4 * D]
    scale_two = own_mod[:, 4 * D : 5 * D]
    gate_two = own_mod[:, 5 * D :]
    freqs = 10000.0 ** (-jnp.arange(HALF, dtype=f32) * 2.0 / HEAD_DIM)
    starts = jnp.stack([(1 - split) * (seat ^ m) * rows for m in seq_masks])
    pos = (starts[:, None] + jnp.arange(rows, dtype=jnp.int32)[None]).astype(f32)
    angles = pos[:, None, :] * freqs[None, :, None]
    cos, sin = jnp.cos(angles), jnp.sin(angles)
    long = (1 - split).reshape(1)

    kinds = 4
    per_seat = batch_size // kinds
    moves = []
    for j in range(world):
        kind, r = divmod(j, world // kinds)
        s, low = divmod(r, per_seat)
        moves.append((j, (kind * per_seat + low) * seq_size + s))
    att_piece = lax.ppermute(attention_master.T.astype(bf16), ALL, moves)
    att_a = gather_rel(att_piece[None, :half], far_first)
    att_b = gather_rel(att_piece[None, half:], near_first)
    at_a = jnp.array(places_of(far_first, 1, batch_size), jnp.int32)
    at_b = jnp.array(places_of(near_first, 1, batch_size), jnp.int32)
    order = jnp.arange(batch_size, dtype=jnp.int32) ^ place
    pa, pb = at_a[order], at_b[order]
    h1_all, qkv, qkv_w = qkv_call(pa, pb, x_all, gain_rows, shift_rows, att_a, att_b, cos, sin)

    wo_ids = range(3 * per_seat, kinds * per_seat)
    wo_own = jnp.concatenate(
        [
            lax.dynamic_index_in_dim(src, at[k], 0, keepdims=False)
            for k in wo_ids
            for src, at in ((att_a, pa), (att_b, pb))
        ],
        axis=0,
    )
    wo_rel = gather_rel(wo_own[None], seq_stages)
    seq_at = jnp.array(places_of(seq_stages, seq_size, seq_size), jnp.int32)
    seq_order = seq_at[jnp.arange(seq_size, dtype=jnp.int32) ^ seat]
    wo_t = wo_rel[seq_order].reshape(D, D)

    up_t = feedforward_master[0].T.astype(bf16)
    down_t = feedforward_master[1].T.astype(bf16)
    both = jnp.concatenate([up_t, down_t], axis=1)
    y_stage, core_stage = seq_stages[:-1], seq_stages[-1:]
    stages_a = far_first + y_stage + core_stage
    stages_b = y_stage + far_first + core_stage
    ff_a = gather_rel(both[None, :half], stages_a).reshape(world * half, 2 * D)
    ff_b = gather_rel(both[None, half:], stages_b).reshape(world * half, 2 * D)
    masks_a = jnp.array(masks_of(stages_a, seq_size), jnp.int32)
    masks_b = jnp.array(masks_of(stages_b, seq_size), jnp.int32)
    bias_up_rows = bias_up.reshape(world, chunk)
    bias_a = bias_up_rows[:, :half][masks_a ^ me].reshape(-1)
    bias_b = bias_up_rows[:, half:][masks_b ^ me].reshape(-1)

    o_all, o_f, lse = forward_call(long, qkv, heads)
    o_parts = [o_all[0]] + [
        lax.ppermute(o_all[k], "seq", [(i, i ^ seq_masks[k]) for i in range(seq_size)])
        for k in range(1, seq_size)
    ]
    o_t = jnp.stack(o_parts)[seq_order].reshape(D, rows)
    attn_out = mm(o_t, wo_t, 0, 1)
    inputs_f = tokens.astype(f32)
    middle = inputs_f + gate_one * attn_out

    centre = middle - jnp.mean(middle, axis=-1, keepdims=True)
    rstd_two = lax.rsqrt(jnp.mean(centre * centre, axis=-1, keepdims=True) + norm_eps)
    n_two = centre * rstd_two
    gain_two_all = gain_two * (1.0 + scale_two)
    h2 = (n_two * gain_two_all + shift_two).astype(bf16)
    grad_out = cotangent.astype(f32)
    gm = (grad_out * gate_two).astype(bf16)
    ffn_out = bias_down
    grad_h2 = 0.0
    weight_grads = []
    bias_grads = []
    halves = []
    for weights, bias in ((ff_a, bias_a), (ff_b, bias_b)):
        w_up, w_down = weights[:, :D], weights[:, D:]
        up_vals = mm(h2, w_up, 1, 1) + bias
        act, gelu_back = jax.vjp(partial(jax.nn.gelu, approximate=True), up_vals)
        act_low = act.astype(bf16)
        ffn_out = ffn_out + mm(act_low, w_down, 1, 0)
        halves.append((w_up, w_down, act_low, gelu_back))
    block_output = (middle + gate_two * ffn_out).astype(bf16)
    for w_up, w_down, act_low, gelu_back in halves:
        dup = gelu_back(mm(gm, w_down, 1, 1))[0].astype(bf16)
        bias_grads.append(jnp.sum(dup.astype(f32), axis=0))
        grad_h2 = grad_h2 + mm(dup, w_up, 1, 0)
        d_up = mm(dup, h2, 0, 0).astype(bf16)
        d_down = mm(act_low, gm, 0, 0).astype(bf16)
        weight_grads.append(jnp.concatenate([d_up, d_down], axis=1))
    grad_bias_down = jnp.sum(gm.astype(f32), axis=0)
    dgt2 = jnp.sum(grad_out * ffn_out, axis=0)
    dsh2 = jnp.sum(grad_h2, axis=0)
    hn2 = jnp.sum(grad_h2 * n_two, axis=0)
    dsc2 = hn2 * gain_two
    dg2 = hn2 * (1.0 + scale_two[0])
    dn = grad_h2 * gain_two_all
    grad_middle = grad_out + rstd_two * (
        dn
        - jnp.mean(dn, axis=-1, keepdims=True)
        - n_two * jnp.mean(dn * n_two, axis=-1, keepdims=True)
    )
    dgt1 = jnp.sum(grad_middle * attn_out, axis=0)
    ga = (grad_middle * gate_one).astype(bf16)
    do_t = mm(wo_t, ga, 0, 1).astype(bf16).reshape(seq_size, heads * HEAD_DIM, rows)
    do_rel = do_t[jnp.array(seq_masks, jnp.int32) ^ seat]
    do_all = jnp.stack(
        [do_rel[0]]
        + [
            lax.ppermute(do_rel[k], "seq", [(i, i ^ seq_masks[k]) for i in range(seq_size)])
            for k in range(1, seq_size)
        ]
    )
    d_wo = mm(ga, o_t, 0, 1).astype(bf16).reshape(seq_size, D // seq_size, D)
    ff_sum_a = scatter_rel(weight_grads[0].reshape(world, half, 2 * D), stages_a)[0]
    ff_sum_b = scatter_rel(weight_grads[1].reshape(world, half, 2 * D), stages_b)[0]
    wo_sum = scatter_rel(d_wo[jnp.array(seq_masks, jnp.int32) ^ seat], seq_stages)[0]

    dq, dk, dv = backward_call(long, qkv, do_all, o_f, lse, cos, sin, heads)
    grad_h1_all, d_qkv_w = qkv_back_call(dq, dk, dv, h1_all, qkv_w)
    att_grad = jnp.concatenate([d_qkv_w, wo_sum], axis=0).reshape(batch_size, chunk, D)
    grad_a = att_grad[:, :half][jnp.array(masks_of(far_first, 1), jnp.int32) ^ place]
    grad_b = att_grad[:, half:][jnp.array(masks_of(near_first, 1), jnp.int32) ^ place]
    att_sum = jnp.concatenate(
        [scatter_rel(grad_a, far_first)[0], scatter_rel(grad_b, near_first)[0]], axis=0
    )
    att_sum = lax.ppermute(att_sum, ALL, [(b, a) for a, b in moves])

    grad_h1 = scatter_rel(grad_h1_all, seq_stages)[0].astype(f32)
    centre = inputs_f - jnp.mean(inputs_f, axis=-1, keepdims=True)
    rstd_one = lax.rsqrt(jnp.mean(centre * centre, axis=-1, keepdims=True) + norm_eps)
    n_one = centre * rstd_one
    dsh1 = jnp.sum(grad_h1, axis=0)
    hn1 = jnp.sum(grad_h1 * n_one, axis=0)
    dsc1 = hn1 * gain_one
    dg1 = hn1 * (1.0 + scale_one[0])
    dn = grad_h1 * (gain_one * (1.0 + scale_one))
    input_grad = grad_middle + rstd_one * (
        dn
        - jnp.mean(dn, axis=-1, keepdims=True)
        - n_one * jnp.mean(dn * n_one, axis=-1, keepdims=True)
    )
    input_grad = input_grad.astype(bf16)

    dmod = jnp.concatenate([dsh1, dsc1, dgt1, dsh2, dsc2, dgt2])
    order_a = jnp.array(places_of(stages_a, seq_size, world), jnp.int32)
    order_b = jnp.array(places_of(stages_b, seq_size, world), jnp.int32)
    devices = jnp.arange(world, dtype=jnp.int32) ^ me
    bias_grad = jnp.concatenate(
        [
            bias_grads[0].reshape(world, half)[order_a[devices]],
            bias_grads[1].reshape(world, half)[order_b[devices]],
        ],
        axis=1,
    ).reshape(-1)
    vec_grad = jnp.concatenate([dg1, dg2, bias_grad, grad_bias_down, dmod])
    tail = jnp.concatenate(
        [dmod.reshape(world, mod_part), vec_grad.reshape(world, vec_part)], axis=1
    )
    tail_all = lax.all_to_all(tail[:, None], ALL, 0, 0, tiled=True)[:, 0]
    vector_sum = jnp.sum(tail_all[:, mod_part:], axis=0)
    slots = jnp.arange(seq_size, dtype=jnp.int32)[None, :] * split_all[:, None].astype(jnp.int32)
    rows_of = (jnp.arange(batch_size, dtype=jnp.int32)[:, None] * SLOTS + slots).reshape(-1)
    cs_dev = cs_all[rows_of].astype(f32)
    adaptive_sum = lax.dot_general(
        cs_dev, tail_all[:, :mod_part], (((0,), (0,)), ((), ())), precision=lax.Precision.HIGHEST
    )

    attention_sum = att_sum.astype(f32).T
    ff_sum = jnp.concatenate([ff_sum_a, ff_sum_b], axis=0).astype(f32)
    forward_sum = jnp.stack([ff_sum[:, :D].T, ff_sum[:, D:].T])
    adaptive_res = adamw_update(
        adaptive_master, adaptive_first, adaptive_second, adaptive_sum, rate_adaptive
    )
    attention_res = adamw_update(
        attention_master, attention_first, attention_second, attention_sum, rate_attention
    )
    forward_res = adamw_update(
        feedforward_master, feedforward_first, feedforward_second, forward_sum, rate_forward
    )
    vector_res = adamw_update(vector_master, vector_first, vector_second, vector_sum, rate_vector)
    return (block_output, input_grad, *adaptive_res, *attention_res, *forward_res, *vector_res)


def solution(mesh):
    rows = P(ALL, None)
    cols = P(None, ALL)
    deep = P(None, None, ALL)
    flat = P(ALL)
    return jax.shard_map(
        on_device,
        mesh=mesh,
        in_specs=(rows, rows, P("batch", None), P("batch")) + (cols, cols, deep, flat) * 3,
        out_specs=(rows, rows) + (cols,) * 8 + (deep,) * 4 + (flat,) * 4,
        check_vma=False,
    )
```

```python
import math

import jax
import jax.numpy as jnp
from jax import lax
from jax.experimental import pallas as pl
from jax.experimental.pallas import tpu as pltpu
from jax.sharding import PartitionSpec as P


D = 768
HEADS = 12
HEAD_DIM = 64
HALF = 32
FF = 3072
COND = 128
SLOTS = 4
STEP = 10
ALL = ("batch", "seq")

beta_one = 0.9
beta_two = 0.999
adam_eps = 1e-08
decay_rate = 0.1
norm_eps = 1e-06
rate_adaptive = 0.15
rate_attention = 0.08
rate_forward = 0.07
rate_vector = 0.4
bf16 = jnp.bfloat16
f32 = jnp.float32
EXPO = math.log2(math.e) * 0.125


def mm(a, b, ca, cb):
    return lax.dot_general(a, b, (((ca,), (cb,)), ((), ())), preferred_element_type=f32)


def swap(v, stage):
    axis, bit = stage
    size = lax.axis_size(axis)
    return lax.ppermute(v, axis, [(i, i ^ bit) for i in range(size)])


def gather_rel(v, stages):
    for stage in stages:
        got = swap(v, stage)
        v = jnp.concatenate([v, got], axis=0)
    return v


def add_low(a, b):
    return (a.astype(f32) + b.astype(f32)).astype(bf16)


def scatter_two(keep, send, stages):
    for n, stage in enumerate(reversed(stages)):
        got = swap(send, stage)
        half = keep.shape[0] // 2
        if n == len(stages) - 1:
            return add_low(keep, got)
        send = add_low(keep[half:], got[half:])
        keep = add_low(keep[:half], got[:half])


def scatter_rel(v, stages):
    half = v.shape[0] // 2
    return scatter_two(v[:half], v[half:], stages)


def flip(v, index):
    shape = v.shape
    for b in range(shape[0].bit_length() - 1):
        w = v.reshape((shape[0] >> (b + 1), 2, 1 << b) + shape[1:])
        swapped = jnp.concatenate([w[:, 1:], w[:, :1]], axis=1)
        v = jnp.where(((index >> b) & 1) == 1, swapped, w).reshape(shape)
    return v


def place_of(mask, stages, seq_size):
    out = 0
    for n, (axis, bit) in enumerate(stages):
        whole = bit * seq_size if axis == "batch" else bit
        out = out + (((mask >> (whole.bit_length() - 1)) & 1) << n)
    return out


def one_hot_pick(index, v, precision=None):
    pick = (index[:, None] == jnp.arange(v.shape[0], dtype=jnp.int32)[None]).astype(f32)
    return jnp.dot(pick, v, precision=precision)


def masks_of(stages, seq_size):
    out = [0]
    for axis, bit in stages:
        whole = bit * seq_size if axis == "batch" else bit
        out = out + [m | whole for m in out]
    return out


def places_of(stages, seq_size, count):
    masks = masks_of(stages, seq_size)
    where = [0] * count
    for k, m in enumerate(masks):
        where[m] = k
    return where


def bits_down(size):
    return [1 << i for i in reversed(range(size.bit_length() - 1))]


def adamw_update(master, first, second, grad, rate):
    first_new = beta_one * first + (1.0 - beta_one) * grad
    second_new = beta_two * second + (1.0 - beta_two) * grad * grad
    first_hat = first_new / (1.0 - beta_one**STEP)
    second_hat = second_new / (1.0 - beta_two**STEP)
    master_new = master - rate * (
        first_hat / (jnp.sqrt(second_hat) + adam_eps) + decay_rate * master
    )
    return (master_new, first_new, second_new, master_new.astype(bf16))


def rope(v, cos, sin):
    v1, v2 = v[:HALF], v[HALF:]
    return jnp.concatenate([v1 * cos - v2 * sin, v2 * cos + v1 * sin], axis=0)


def rope_back(v, cos, sin):
    v1, v2 = v[:HALF], v[HALF:]
    return jnp.concatenate([v1 * cos + v2 * sin, v2 * cos - v1 * sin], axis=0)


def qkv_kernel(pa, pb, x_ref, gain_ref, shift_ref, wa_ref, wb_ref, cos_ref, sin_ref, h_ref, q_ref, w_ref):
    part = wa_ref.shape[1]
    chunks = w_ref.shape[0] // (2 * part)

    @pl.when(pl.program_id(0) == 0)
    def _():
        for k in range(chunks):
            w_ref[2 * part * k : 2 * part * k + part, :] = wa_ref[pa[k]]
            w_ref[2 * part * k + part : 2 * part * (k + 1), :] = wb_ref[pb[k]]

    x = x_ref[0].astype(f32)
    mean = jnp.mean(x, axis=-1, keepdims=True)
    centre = x - mean
    var = jnp.mean(centre * centre, axis=-1, keepdims=True)
    h = centre * lax.rsqrt(var + norm_eps) * gain_ref[0] + shift_ref[0]
    h = h.astype(bf16)
    h_ref[0] = h
    out = mm(w_ref[...], h, 1, 1)
    cos, sin = cos_ref[0], sin_ref[0]
    rows = out.shape[0] // 3
    for i in range(2 * rows // HEAD_DIM):
        at = i * HEAD_DIM
        q_ref[0, at : at + HEAD_DIM, :] = rope(out[at : at + HEAD_DIM], cos, sin).astype(bf16)
    q_ref[0, 2 * rows :, :] = out[2 * rows :].astype(bf16)


def split_two(v):
    hi = v.astype(bf16)
    return hi, (v - hi.astype(f32)).astype(bf16)


def three_rows(v, rows):
    a = v.astype(bf16).astype(f32)
    b = (v - a).astype(bf16).astype(f32)
    c = v - a - b
    at = lax.broadcasted_iota(jnp.int32, (rows, v.shape[1]), 0)
    out = jnp.where(at == 0, a, jnp.where(at == 1, b, jnp.where(at == 2, c, 0.0)))
    return out.astype(bf16)


def forward_kernel(long_ref, q_ref, k_ref, v_ref, o_ref, of_ref, l_ref, kk):
    blocks, _, rows = k_ref.shape
    qb = pl.program_id(1)

    @pl.when(qb == 0)
    def _():
        for r in range(blocks):
            k = k_ref[r]
            kk[r * rows : (r + 1) * rows, :] = jnp.concatenate([k, k], axis=0).T

    hi, lo = split_two(q_ref[0].astype(f32) * EXPO)
    query = jnp.concatenate([hi, lo], axis=0)

    def finish(out, total, top):
        out = out / total
        of_ref[0] = out
        o_ref[0] = out.astype(bf16)
        l_ref[0, 0] = top + jnp.log2(total)

    @pl.when(long_ref[0] == 1)
    def _():
        scores = [mm(kk[r * rows : (r + 1) * rows, :], query, 1, 0) for r in range(blocks)]
        top = jnp.max(scores[0], axis=0, keepdims=True)
        for s in scores[1:]:
            top = jnp.maximum(top, jnp.max(s, axis=0, keepdims=True))
        out = jnp.zeros((HEAD_DIM, rows), f32)
        total = jnp.zeros((1, rows), f32)
        for r in range(blocks):
            e = jnp.exp2(scores[r] - top)
            total = total + jnp.sum(e, axis=0, keepdims=True)
            out = out + mm(v_ref[r], e.astype(bf16), 1, 0)
        finish(out, total, top)

    @pl.when(long_ref[0] == 0)
    def _():
        start = pl.multiple_of(qb * rows, rows)
        s = mm(kk[pl.ds(start, rows), :], query, 1, 0)
        top = jnp.max(s, axis=0, keepdims=True)
        e = jnp.exp2(s - top)
        total = jnp.sum(e, axis=0, keepdims=True)
        finish(mm(v_ref[qb], e.astype(bf16), 1, 0), total, top)


def backward_kernel(
    long_ref, q_ref, k_ref, v_ref, do_ref, of_ref, l_ref, cos_ref, sin_ref,
    dq_ref, dk_ref, dv_ref, kk, vv, dk, dv,
):
    blocks, _, rows = k_ref.shape
    qb = pl.program_id(1)

    @pl.when(qb == 0)
    def _():
        for r in range(blocks):
            k, v = k_ref[r], v_ref[r]
            one = jnp.ones((HEAD_DIM, rows), bf16)
            span = slice(r * rows, (r + 1) * rows)
            kk[span, :] = jnp.concatenate([k, k, one, one], axis=0).T
            vv[span, :] = jnp.concatenate([v, one], axis=0).T
        dk[...] = jnp.zeros_like(dk)
        dv[...] = jnp.zeros_like(dv)

    q = q_ref[0]
    do = do_ref[0]
    hi, lo = split_two(q.astype(f32) * EXPO)
    query = jnp.concatenate([hi, lo, three_rows(-l_ref[0, 0], 2 * HEAD_DIM)], axis=0)
    delta = jnp.sum(do.astype(f32) * of_ref[0], axis=0, keepdims=True)
    grad = jnp.concatenate([do, three_rows(-delta, HEAD_DIM)], axis=0)
    q_rows = q.T
    do_rows = do.T
    cos, sin = cos_ref[qb], sin_ref[qb]

    def one(start, k):
        span = pl.ds(start, rows)
        p = jnp.exp2(mm(kk[span, :], query, 1, 0))
        ds = (p * mm(vv[span, :], grad, 1, 0)).astype(bf16)
        dv[span, :] += mm(p.astype(bf16), do_rows, 1, 0)
        dk[span, :] += mm(ds, q_rows, 1, 0)
        return mm(k, ds, 1, 0)

    def finish(total):
        dq_ref[0] = rope_back(total * 0.125, cos, sin).astype(bf16)

    @pl.when(long_ref[0] == 1)
    def _():
        total = one(0, k_ref[0])
        for r in range(1, blocks):
            total = total + one(r * rows, k_ref[r])
        finish(total)

    @pl.when(long_ref[0] == 0)
    def _():
        finish(one(pl.multiple_of(qb * rows, rows), k_ref[qb]))

    @pl.when(qb == blocks - 1)
    def _():
        for r in range(blocks):
            span = slice(r * rows, (r + 1) * rows)
            dk_ref[r] = rope_back(dk[span, :].T * 0.125, cos_ref[r], sin_ref[r]).astype(bf16)
            dv_ref[r] = dv[span, :].T.astype(bf16)


def grad_h_kernel(*refs):
    parts, w_ref, dh_ref = refs[:-2], refs[-2], refs[-1]
    g = jnp.concatenate([r[0] for r in parts], axis=0)
    dh_ref[0] = mm(g.T, w_ref[...], 1, 0).astype(bf16)


def grad_w_kernel(*refs):
    parts, h_ref, dw_ref, acc = refs[:-3], refs[-3], refs[-2], refs[-1]
    b = pl.program_id(0)
    g = jnp.concatenate([r[0] for r in parts], axis=0)
    dw = mm(g, h_ref[0], 1, 0)

    @pl.when(b == 0)
    def _():
        acc[...] = dw

    @pl.when(b > 0)
    def _():
        acc[...] += dw

    @pl.when(b == pl.num_programs(0) - 1)
    def _():
        dw_ref[...] = acc[...].astype(bf16)


def ffn_kernel(
    h_ref, g_ref, mo_in, dh_in, wm_ref, wt_ref, bm_ref, bt_ref,
    mo_ref, dh_ref, dwm_ref, dwt_ref, dbm_ref, dbt_ref, h_t, g_t,
):
    i = pl.program_id(0)
    half = pl.num_programs(0) // 2

    @pl.when(i == 0)
    def _():
        h_t[...] = h_ref[...].T
        g_t[...] = g_ref[...].T
        mo_ref[...] = mo_in[...]
        dh_ref[...] = dh_in[...]

    def one(w_ref, b_ref, dw_ref, db_ref):
        w_up, w_down = w_ref[:, :D], w_ref[:, D:]
        rows = w_up.shape[0]
        bias = jnp.broadcast_to(b_ref[...], (128, rows)).T[:, :1]
        up = mm(w_up, h_t[...], 1, 0) + bias
        root = math.sqrt(2.0 / math.pi)
        square = up * up
        t = jnp.tanh(root * up * (1.0 + 0.044715 * square))
        half_t = 0.5 + 0.5 * t
        act = (up * half_t).astype(bf16)
        slope = half_t + 0.5 * up * (1.0 - t * t) * (root * (1.0 + 3.0 * 0.044715 * square))
        dup = (mm(w_down, g_t[...], 1, 0) * slope).astype(bf16)
        dw_ref[:, :D] = mm(dup, h_ref[...], 1, 0).astype(bf16)
        dw_ref[:, D:] = mm(act, g_ref[...], 1, 0).astype(bf16)
        dup_t = dup.T
        mo_ref[...] += mm(act.T, w_down, 1, 0)
        dh_ref[...] += mm(dup_t, w_up, 1, 0)
        db_ref[...] = mm(jnp.ones((16, dup_t.shape[0]), bf16), dup_t, 1, 0)[:1]

    @pl.when(i < half)
    def _():
        one(wt_ref, bt_ref, dwt_ref, dbt_ref)

    @pl.when(i >= half)
    def _():
        one(wm_ref, bm_ref, dwm_ref, dbm_ref)


def full(shape):
    return pl.BlockSpec(shape, lambda *_: (0,) * len(shape))


SMEM = pl.BlockSpec(memory_space=pltpu.SMEM)
ONE = pltpu.CompilerParams(dimension_semantics=("arbitrary",))
TWO = pltpu.CompilerParams(dimension_semantics=("arbitrary", "arbitrary"))


def qkv_call(pa, pb, x, gain, shift, wa, wb, cos, sin):
    blocks, rows, _ = x.shape
    feats = 3 * wa.shape[0] * (wa.shape[1] + wb.shape[1]) // 4
    block = lambda *s: pl.BlockSpec((1,) + s, lambda b: (b, 0, 0))
    return pl.pallas_call(
        qkv_kernel,
        name="qkv",
        grid=(blocks,),
        in_specs=[SMEM, SMEM, block(rows, D), block(1, D), block(1, D), full(wa.shape), full(wb.shape), block(HALF, rows), block(HALF, rows)],
        out_specs=[block(rows, D), block(feats, rows), full((feats, D))],
        out_shape=[
            jax.ShapeDtypeStruct((blocks, rows, D), bf16),
            jax.ShapeDtypeStruct((blocks, feats, rows), bf16),
            jax.ShapeDtypeStruct((feats, D), bf16),
        ],
        compiler_params=ONE,
    )(pa, pb, x, gain, shift, wa, wb, cos, sin)


def forward_call(long, qkv, heads, head):
    blocks, _, rows = qkv.shape
    part = lambda n: pl.BlockSpec((blocks, HEAD_DIM, rows), lambda h, b, n=n: (0, n * heads + head, 0))
    own = pl.BlockSpec((1, HEAD_DIM, rows), lambda h, b: (b, head, 0))
    out = pl.BlockSpec((1, HEAD_DIM, rows), lambda h, b: (b, 0, 0))
    return pl.pallas_call(
        forward_kernel,
        name="attn_fwd",
        grid=(1, blocks),
        in_specs=[SMEM, own, part(1), part(2)],
        out_specs=[out, out, pl.BlockSpec((1, 1, 1, rows), lambda h, b: (0, b, 0, 0))],
        out_shape=[
            jax.ShapeDtypeStruct((blocks, HEAD_DIM, rows), bf16),
            jax.ShapeDtypeStruct((blocks, HEAD_DIM, rows), f32),
            jax.ShapeDtypeStruct((1, blocks, 1, rows), f32),
        ],
        scratch_shapes=[pltpu.VMEM((blocks * rows, 2 * HEAD_DIM), bf16)],
        compiler_params=TWO,
    )(long, qkv, qkv, qkv)


def backward_call(long, qkv, do, of, lse, cos, sin, heads, head):
    blocks, _, rows = qkv.shape
    part = lambda n: pl.BlockSpec((blocks, HEAD_DIM, rows), lambda h, b, n=n: (0, n * heads + head, 0))
    own = pl.BlockSpec((1, HEAD_DIM, rows), lambda h, b: (b, head, 0))
    out = pl.BlockSpec((1, HEAD_DIM, rows), lambda h, b: (b, 0, 0))
    whole = pl.BlockSpec((blocks, HEAD_DIM, rows), lambda h, b: (0, 0, 0))
    shape = jax.ShapeDtypeStruct((blocks, HEAD_DIM, rows), bf16)
    return pl.pallas_call(
        backward_kernel,
        name="attn_bwd",
        grid=(1, blocks),
        in_specs=[SMEM, own, part(1), part(2), own, out, pl.BlockSpec((1, 1, 1, rows), lambda h, b: (0, b, 0, 0)), full(cos.shape), full(sin.shape)],
        out_specs=[out, whole, whole],
        out_shape=[shape, shape, shape],
        scratch_shapes=[
            pltpu.VMEM((blocks * rows, 4 * HEAD_DIM), bf16),
            pltpu.VMEM((blocks * rows, 2 * HEAD_DIM), bf16),
            pltpu.VMEM((blocks * rows, HEAD_DIM), f32),
            pltpu.VMEM((blocks * rows, HEAD_DIM), f32),
        ],
        compiler_params=TWO,
    )(long, qkv, qkv, qkv, do, of, lse, cos, sin)


def grad_h_call(parts, w):
    blocks, feats, rows = parts[0].shape
    back = lambda *s: pl.BlockSpec((1,) + s, lambda b: (blocks - 1 - b, 0, 0))
    return pl.pallas_call(
        grad_h_kernel,
        name="grad_h",
        grid=(blocks,),
        in_specs=[back(feats, rows)] * len(parts) + [full(w.shape)],
        out_specs=back(rows, D),
        out_shape=jax.ShapeDtypeStruct((blocks, rows, D), bf16),
        compiler_params=ONE,
    )(*parts, w)


def grad_w_call(parts, h):
    blocks, feats, rows = parts[0].shape
    block = lambda *s: pl.BlockSpec((1,) + s, lambda b: (b, 0, 0))
    shape = (feats * len(parts), D)
    return pl.pallas_call(
        grad_w_kernel,
        name="grad_w",
        grid=(blocks,),
        in_specs=[block(feats, rows)] * len(parts) + [block(rows, D)],
        out_specs=full(shape),
        out_shape=jax.ShapeDtypeStruct(shape, bf16),
        scratch_shapes=[pltpu.VMEM(shape, f32)],
        compiler_params=ONE,
    )(*parts, h)


def ffn_call(h, g, mo, dh, mine, theirs, bias_mine, bias_theirs):
    rows = h.shape[0]
    hidden = mine.shape[0]
    tiles = 2
    tile = hidden // tiles
    first = lambda i: jnp.minimum(i, tiles - 1)
    second = lambda i: jnp.maximum(i - tiles, 0)
    wide = lambda f: pl.BlockSpec((tile, 2 * D), lambda i: (f(i), 0))
    flat = lambda f: pl.BlockSpec((1, tile), lambda i: (0, f(i)))
    token = full((rows, D))
    return pl.pallas_call(
        ffn_kernel,
        name="ffn",
        grid=(2 * tiles,),
        in_specs=[token] * 4 + [wide(second), wide(first), flat(second), flat(first)],
        out_specs=[token, token, wide(second), wide(first), flat(second), flat(first)],
        out_shape=[
            jax.ShapeDtypeStruct((rows, D), f32),
            jax.ShapeDtypeStruct((rows, D), f32),
            jax.ShapeDtypeStruct((hidden, 2 * D), bf16),
            jax.ShapeDtypeStruct((hidden, 2 * D), bf16),
            jax.ShapeDtypeStruct((1, hidden), f32),
            jax.ShapeDtypeStruct((1, hidden), f32),
        ],
        scratch_shapes=[pltpu.VMEM((D, rows), bf16), pltpu.VMEM((D, rows), bf16)],
        compiler_params=ONE,
    )(h, g, mo, dh, mine, theirs, bias_mine, bias_theirs)


def on_device(
    tokens, cotangent, cond, seq_lengths,
    adaptive_master, attention_master, feedforward_master, vector_master,
    adaptive_first, attention_first, feedforward_first, vector_first,
    adaptive_second, attention_second, feedforward_second, vector_second,
):
    rows = tokens.shape[0]
    seq_size = lax.axis_size("seq")
    batch_size = lax.axis_size("batch")
    world = seq_size * batch_size
    heads = HEADS // seq_size
    seat = lax.axis_index("seq")
    place = lax.axis_index("batch")
    me = place * seq_size + seat
    seq_stages = [("seq", b) for b in bits_down(seq_size)]
    batch_bits = bits_down(batch_size)
    far_first = [("batch", b) for b in batch_bits]
    near_first = [("batch", batch_bits[-1])] + [("batch", b) for b in batch_bits[:-1]]
    seq_masks = masks_of(seq_stages, seq_size)
    chunk = attention_master.shape[1]
    half = chunk // 2

    cs = jax.nn.silu(cond.astype(f32)).astype(bf16)
    split = (seq_lengths[1] > 0).astype(jnp.int32)
    vec_part = vector_master.shape[0]
    vec_rows = -(-vec_part // COND)
    vec_pad = jnp.pad(vector_master.astype(bf16), (0, vec_rows * COND - vec_part))
    flag = jnp.full((1, COND), 1.0, bf16) * split.astype(bf16)
    small = jnp.concatenate([cs, flag, vec_pad.reshape(vec_rows, COND)], axis=0)
    small = jnp.broadcast_to(small[None], (world,) + small.shape)
    small_all = lax.all_to_all(small, ALL, 0, 0, tiled=True)
    cs_all = small_all[::seq_size, :SLOTS].reshape(batch_size * SLOTS, COND)
    split_all = small_all[::seq_size, SLOTS, 0] > 0
    vector_f = small_all[:, SLOTS + 1 :].reshape(world, vec_rows * COND)[:, :vec_part]
    vector_f = vector_f.reshape(-1).astype(f32)
    gain_one = vector_f[:D]
    gain_two = vector_f[D : 2 * D]
    bias_up = vector_f[2 * D : 2 * D + FF]
    bias_down = vector_f[2 * D + FF : 3 * D + FF]
    bias_mod = vector_f[3 * D + FF :]
    mod_part = adaptive_master.shape[1]
    mod_cols = mm(cs_all, adaptive_master.astype(bf16), 1, 0)
    mod_send = jnp.broadcast_to(
        mod_cols.reshape(batch_size, 1, SLOTS, mod_part), (batch_size, seq_size, SLOTS, mod_part)
    ).reshape(world, SLOTS, mod_part)
    mod_got = lax.all_to_all(mod_send, ALL, 0, 0, tiled=True)
    mod = jnp.swapaxes(mod_got, 0, 1).reshape(SLOTS, world * mod_part) + bias_mod

    x_all = gather_rel(tokens[None], seq_stages)
    slot_of = [split * (seat ^ m) for m in seq_masks]
    mod_here = [lax.dynamic_index_in_dim(mod, s, 0, keepdims=True) for s in slot_of]
    gain_rows = jnp.stack([gain_one * (1.0 + m[:, D : 2 * D]) for m in mod_here])
    shift_rows = jnp.stack([m[:, :D] for m in mod_here])
    own_mod = mod_here[0]
    scale_one = own_mod[:, D : 2 * D]
    gate_one = own_mod[:, 2 * D : 3 * D]
    shift_two = own_mod[:, 3 * D : 4 * D]
    scale_two = own_mod[:, 4 * D : 5 * D]
    gate_two = own_mod[:, 5 * D :]
    freqs = 10000.0 ** (-jnp.arange(HALF, dtype=f32) * 2.0 / HEAD_DIM)
    starts = jnp.stack([(1 - split) * (seat ^ m) * rows for m in seq_masks])
    pos = (starts[:, None] + jnp.arange(rows, dtype=jnp.int32)[None]).astype(f32)
    angles = pos[:, None, :] * freqs[None, :, None]
    cos, sin = jnp.cos(angles), jnp.sin(angles)
    long = (1 - split).reshape(1)

    kinds = 4
    per_seat = batch_size // kinds
    moves = []
    for j in range(world):
        kind, r = divmod(j, world // kinds)
        s, low = divmod(r, per_seat)
        moves.append((j, (kind * per_seat + low) * seq_size + s))
    att_piece = lax.ppermute(attention_master.T.astype(bf16), ALL, moves)
    att_a = gather_rel(att_piece[None, :half], far_first)
    att_b = gather_rel(att_piece[None, half:], near_first)
    order = jnp.arange(batch_size, dtype=jnp.int32) ^ place
    pa, pb = place_of(order, far_first, 1), place_of(order, near_first, 1)
    h1_all, qkv, qkv_w = qkv_call(pa, pb, x_all, gain_rows, shift_rows, att_a, att_b, cos, sin)

    wo_ids = range(3 * per_seat, kinds * per_seat)
    wo_own = jnp.concatenate(
        [
            lax.dynamic_index_in_dim(src, at[k], 0, keepdims=False)
            for k in wo_ids
            for src, at in ((att_a, pa), (att_b, pb))
        ],
        axis=0,
    )
    wo_rel = gather_rel(wo_own[None], seq_stages)
    to_abs = lambda parts: flip(jnp.stack([parts[k] for k in places_of(seq_stages, seq_size, seq_size)]), seat)
    to_rel = lambda v: [flip(v, seat)[m] for m in seq_masks]
    wo_t = to_abs(wo_rel).reshape(D, D)

    up_t = feedforward_master[0].T.astype(bf16)
    down_t = feedforward_master[1].T.astype(bf16)
    both = jnp.concatenate([up_t, down_t], axis=1)
    y_stage, core_stage = seq_stages[:-1], seq_stages[-1:]
    stages_a = far_first + y_stage + core_stage
    stages_b = y_stage + far_first + core_stage
    ff_a = gather_rel(both[None, :half], stages_a[:-1])
    ff_b = gather_rel(both[None, half:], stages_b[:-1])
    wide = lambda v: v.reshape(-1, 2 * D)
    ff_a2 = wide(swap(ff_a, core_stage[0]))
    ff_b2 = wide(swap(ff_b, core_stage[0]))
    ff_a, ff_b = wide(ff_a), wide(ff_b)
    masks_a = jnp.array(masks_of(stages_a, seq_size), jnp.int32)
    masks_b = jnp.array(masks_of(stages_b, seq_size), jnp.int32)
    bias_up_rows = bias_up.reshape(world, chunk)
    bias_a = one_hot_pick(masks_a ^ me, bias_up_rows[:, :half]).reshape(2, -1)
    bias_b = one_hot_pick(masks_b ^ me, bias_up_rows[:, half:]).reshape(2, -1)

    def spread(parts):
        return [parts[0]] + [swap(parts[k], ("seq", seq_masks[k])) for k in range(1, seq_size)]

    kept = []
    o_heads = []
    for n in range(heads):
        o_n, o_f, lse = forward_call(long, qkv, heads, n)
        kept.append((o_f, lse))
        o_heads.append(spread(o_n))
    o_parts = [jnp.concatenate([h[k] for h in o_heads], axis=0) for k in range(seq_size)]
    o_t = to_abs(o_parts).reshape(D, rows)
    attn_out = mm(o_t, wo_t, 0, 1)
    inputs_f = tokens.astype(f32)
    middle = inputs_f + gate_one * attn_out

    centre = middle - jnp.mean(middle, axis=-1, keepdims=True)
    rstd_two = lax.rsqrt(jnp.mean(centre * centre, axis=-1, keepdims=True) + norm_eps)
    n_two = centre * rstd_two
    gain_two_all = gain_two * (1.0 + scale_two)
    h2 = (n_two * gain_two_all + shift_two).astype(bf16)
    grad_out = cotangent.astype(f32)
    gm = (grad_out * gate_two).astype(bf16)
    mo = jnp.broadcast_to(bias_down[None], (rows, D))
    grad_h2 = jnp.zeros((rows, D), f32)
    mo, grad_h2, da, da2, db_a, db_a2 = ffn_call(
        h2, gm, mo, grad_h2, ff_a, ff_a2, bias_a[:1], bias_a[1:]
    )
    ffn_out, grad_h2, db, db2, db_b, db_b2 = ffn_call(
        h2, gm, mo, grad_h2, ff_b, ff_b2, bias_b[:1], bias_b[1:]
    )
    block_output = (middle + gate_two * ffn_out).astype(bf16)
    grad_bias_down = jnp.sum(gm.astype(f32), axis=0)
    dgt2 = jnp.sum(grad_out * ffn_out, axis=0)
    dsh2 = jnp.sum(grad_h2, axis=0)
    hn2 = jnp.sum(grad_h2 * n_two, axis=0)
    dsc2 = hn2 * gain_two
    dg2 = hn2 * (1.0 + scale_two[0])
    dn = grad_h2 * gain_two_all
    grad_middle = grad_out + rstd_two * (
        dn
        - jnp.mean(dn, axis=-1, keepdims=True)
        - n_two * jnp.mean(dn * n_two, axis=-1, keepdims=True)
    )
    dgt1 = jnp.sum(grad_middle * attn_out, axis=0)
    ga = (grad_middle * gate_one).astype(bf16)
    do_t = mm(wo_t, ga, 0, 1).astype(bf16).reshape(seq_size, heads * HEAD_DIM, rows)
    do_all = jnp.stack(spread(to_rel(do_t)))
    d_wo = mm(ga, o_t, 0, 1).astype(bf16).reshape(seq_size, D // seq_size, D)
    pieces = lambda v: v.reshape(world // 2, half, 2 * D)
    ff_sum_a = scatter_two(pieces(da), pieces(da2), stages_a)[0]
    ff_sum_b = scatter_two(pieces(db), pieces(db2), stages_b)[0]
    wo_sum = scatter_rel(jnp.stack(to_rel(d_wo)), seq_stages)[0]

    head_grads = []
    for n in range(heads):
        head_grads.append(backward_call(long, qkv, do_all, *kept[n], cos, sin, heads, n))
    parts = [g[k] for k in range(3) for g in head_grads]
    grad_h1_all = grad_h_call(parts, qkv_w)
    d_qkv_w = grad_w_call(parts, h1_all)
    att_grad = jnp.concatenate([d_qkv_w, wo_sum], axis=0).reshape(batch_size, chunk, D)
    att_grad = flip(att_grad, place)
    ordered = lambda v, stages: jnp.stack([v[m] for m in masks_of(stages, 1)])
    att_sum = jnp.concatenate(
        [
            scatter_rel(ordered(att_grad[:, :half], far_first), far_first)[0],
            scatter_rel(ordered(att_grad[:, half:], near_first), near_first)[0],
        ],
        axis=0,
    )
    att_sum = lax.ppermute(att_sum, ALL, [(b, a) for a, b in moves])

    grad_h1 = scatter_rel(grad_h1_all, seq_stages)[0].astype(f32)
    centre = inputs_f - jnp.mean(inputs_f, axis=-1, keepdims=True)
    rstd_one = lax.rsqrt(jnp.mean(centre * centre, axis=-1, keepdims=True) + norm_eps)
    n_one = centre * rstd_one
    dsh1 = jnp.sum(grad_h1, axis=0)
    hn1 = jnp.sum(grad_h1 * n_one, axis=0)
    dsc1 = hn1 * gain_one
    dg1 = hn1 * (1.0 + scale_one[0])
    dn = grad_h1 * (gain_one * (1.0 + scale_one))
    input_grad = grad_middle + rstd_one * (
        dn
        - jnp.mean(dn, axis=-1, keepdims=True)
        - n_one * jnp.mean(dn * n_one, axis=-1, keepdims=True)
    )
    input_grad = input_grad.astype(bf16)

    dmod = jnp.concatenate([dsh1, dsc1, dgt1, dsh2, dsc2, dgt2])
    devices = jnp.arange(world, dtype=jnp.int32) ^ me
    exact = lax.Precision.HIGHEST
    bias_grad = jnp.concatenate(
        [
            one_hot_pick(
                place_of(devices, stages, seq_size),
                jnp.concatenate(d).reshape(world, half),
                exact,
            )
            for d, stages in (((db_a, db_a2), stages_a), ((db_b, db_b2), stages_b))
        ],
        axis=1,
    ).reshape(-1)
    vec_grad = jnp.concatenate([dg1, dg2, bias_grad, grad_bias_down, dmod])
    tail = jnp.concatenate(
        [dmod.reshape(world, mod_part), vec_grad.reshape(world, vec_part)], axis=1
    )
    tail_all = lax.all_to_all(tail[:, None], ALL, 0, 0, tiled=True)[:, 0]
    vector_sum = jnp.sum(tail_all[:, mod_part:], axis=0)
    slots = jnp.arange(seq_size, dtype=jnp.int32)[None, :] * split_all[:, None].astype(jnp.int32)
    rows_of = (jnp.arange(batch_size, dtype=jnp.int32)[:, None] * SLOTS + slots).reshape(-1)
    cs_dev = one_hot_pick(rows_of, cs_all.astype(f32))
    adaptive_sum = lax.dot_general(
        cs_dev, tail_all[:, :mod_part], (((0,), (0,)), ((), ())), precision=lax.Precision.HIGHEST
    )

    attention_sum = att_sum.astype(f32).T
    ff_sum = jnp.concatenate([ff_sum_a, ff_sum_b], axis=0).astype(f32)
    forward_sum = jnp.stack([ff_sum[:, :D].T, ff_sum[:, D:].T])
    adaptive_res = adamw_update(
        adaptive_master, adaptive_first, adaptive_second, adaptive_sum, rate_adaptive
    )
    attention_res = adamw_update(
        attention_master, attention_first, attention_second, attention_sum, rate_attention
    )
    forward_res = adamw_update(
        feedforward_master, feedforward_first, feedforward_second, forward_sum, rate_forward
    )
    vector_res = adamw_update(vector_master, vector_first, vector_second, vector_sum, rate_vector)
    return (block_output, input_grad, *adaptive_res, *attention_res, *forward_res, *vector_res)


def solution(mesh):
    rows = P(ALL, None)
    cols = P(None, ALL)
    deep = P(None, None, ALL)
    flat = P(ALL)
    return jax.shard_map(
        on_device,
        mesh=mesh,
        in_specs=(rows, rows, P("batch", None), P("batch")) + (cols, cols, deep, flat) * 3,
        out_specs=(rows, rows) + (cols,) * 8 + (deep,) * 4 + (flat,) * 4,
        check_vma=False,
    )
```

```python
import math

import jax
import jax.numpy as jnp
from jax import lax
from jax.experimental import pallas as pl
from jax.experimental.pallas import tpu as pltpu
from jax.sharding import PartitionSpec as P


D = 768
HEADS = 12
HEAD_DIM = 64
HALF = 32
FF = 3072
COND = 128
SLOTS = 4
STEP = 10
ALL = ("batch", "seq")

beta_one = 0.9
beta_two = 0.999
adam_eps = 1e-08
decay_rate = 0.1
norm_eps = 1e-06
rate_adaptive = 0.15
rate_attention = 0.08
rate_forward = 0.07
rate_vector = 0.4
bf16 = jnp.bfloat16
f32 = jnp.float32
EXPO = math.log2(math.e) * 0.125


def mm(a, b, ca, cb):
    return lax.dot_general(a, b, (((ca,), (cb,)), ((), ())), preferred_element_type=f32)


def swap(v, stage):
    axis, bit = stage
    size = lax.axis_size(axis)
    return lax.ppermute(v, axis, [(i, i ^ bit) for i in range(size)])


def gather_rel(v, stages):
    for stage in stages:
        got = swap(v, stage)
        v = lax.optimization_barrier(jnp.concatenate([v, got], axis=0))
    return v


def add_low(a, b):
    return (a.astype(f32) + b.astype(f32)).astype(bf16)


def scatter_two(keep, send, stages):
    for n, stage in enumerate(reversed(stages)):
        got = swap(send, stage)
        half = keep.shape[0] // 2
        if n == len(stages) - 1:
            return add_low(keep, got)
        send = add_low(keep[half:], got[half:])
        keep = add_low(keep[:half], got[:half])


def scatter_rel(v, stages):
    half = v.shape[0] // 2
    return scatter_two(v[:half], v[half:], stages)


def flip(v, index):
    shape = v.shape
    for b in range(shape[0].bit_length() - 1):
        w = v.reshape((shape[0] >> (b + 1), 2, 1 << b) + shape[1:])
        swapped = jnp.concatenate([w[:, 1:], w[:, :1]], axis=1)
        v = jnp.where(((index >> b) & 1) == 1, swapped, w).reshape(shape)
    return v


def place_of(mask, stages, seq_size):
    out = 0
    for n, (axis, bit) in enumerate(stages):
        whole = bit * seq_size if axis == "batch" else bit
        out = out + (((mask >> (whole.bit_length() - 1)) & 1) << n)
    return out


def one_hot_pick(index, v, precision=None):
    pick = (index[:, None] == jnp.arange(v.shape[0], dtype=jnp.int32)[None]).astype(f32)
    return jnp.dot(pick, v, precision=precision)


def masks_of(stages, seq_size):
    out = [0]
    for axis, bit in stages:
        whole = bit * seq_size if axis == "batch" else bit
        out = out + [m | whole for m in out]
    return out


def places_of(stages, seq_size, count):
    masks = masks_of(stages, seq_size)
    where = [0] * count
    for k, m in enumerate(masks):
        where[m] = k
    return where


def bits_down(size):
    return [1 << i for i in reversed(range(size.bit_length() - 1))]


def adamw_update(master, first, second, grad, rate):
    first_new = beta_one * first + (1.0 - beta_one) * grad
    second_new = beta_two * second + (1.0 - beta_two) * grad * grad
    first_hat = first_new / (1.0 - beta_one**STEP)
    second_hat = second_new / (1.0 - beta_two**STEP)
    master_new = master - rate * (
        first_hat / (jnp.sqrt(second_hat) + adam_eps) + decay_rate * master
    )
    return (master_new, first_new, second_new, master_new.astype(bf16))


def rope(v, cos, sin):
    v1, v2 = v[:HALF], v[HALF:]
    return jnp.concatenate([v1 * cos - v2 * sin, v2 * cos + v1 * sin], axis=0)


def rope_back(v, cos, sin):
    v1, v2 = v[:HALF], v[HALF:]
    return jnp.concatenate([v1 * cos + v2 * sin, v2 * cos - v1 * sin], axis=0)


def qkv_kernel(pa, pb, xa, xb, xc, xd, gain_ref, shift_ref, wa0, wa1, wb0, wb1, cos_ref, sin_ref, h_ref, q_ref, w_ref, wo_ref, x_ref):
    part = wa0.shape[1]
    chunks = 2 * wa0.shape[0]
    feats = w_ref.shape[0]
    b = pl.program_id(0)

    @pl.when(b == 0)
    def _():
        for k in range(chunks):
            for n, (place, low, high) in enumerate(((pa, wa0, wa1), (pb, wb0, wb1))):
                at = place[k]
                row = at % (chunks // 2)
                piece = jnp.where(at < chunks // 2, low[row], high[row])
                start = (2 * k + n) * part
                if start < feats:
                    w_ref[start : start + part, :] = piece
                else:
                    wo_ref[start - feats : start - feats + part, :] = piece

    for n, ref in enumerate((xa, xb, xc, xd)):

        @pl.when(b == n)
        def _(ref=ref):
            x_ref[...] = ref[0].astype(f32)

    x = x_ref[...]
    mean = jnp.mean(x, axis=-1, keepdims=True)
    centre = x - mean
    var = jnp.mean(centre * centre, axis=-1, keepdims=True)
    h = centre * lax.rsqrt(var + norm_eps) * gain_ref[0] + shift_ref[0]
    h = h.astype(bf16)
    h_ref[0] = h
    out = mm(w_ref[...], h, 1, 1)
    cos, sin = cos_ref[0], sin_ref[0]
    rows = out.shape[0] // 3
    for i in range(2 * rows // HEAD_DIM):
        at = i * HEAD_DIM
        q_ref[0, at : at + HEAD_DIM, :] = rope(out[at : at + HEAD_DIM], cos, sin).astype(bf16)
    q_ref[0, 2 * rows :, :] = out[2 * rows :].astype(bf16)


def split_two(v):
    hi = v.astype(bf16)
    return hi, (v - hi.astype(f32)).astype(bf16)


def three_rows(v, rows):
    a = v.astype(bf16).astype(f32)
    b = (v - a).astype(bf16).astype(f32)
    c = v - a - b
    at = lax.broadcasted_iota(jnp.int32, (rows, v.shape[1]), 0)
    out = jnp.where(at == 0, a, jnp.where(at == 1, b, jnp.where(at == 2, c, 0.0)))
    return out.astype(bf16)


def forward_kernel(long_ref, q_ref, k_ref, v_ref, o_ref, of_ref, l_ref, kk, scores, acc):
    blocks, _, rows = k_ref.shape
    qb = pl.program_id(1)

    @pl.when(qb == 0)
    def _():
        for r in range(blocks):
            k = k_ref[r]
            kk[r * rows : (r + 1) * rows, :] = jnp.concatenate([k, k], axis=0).T

    hi, lo = split_two(q_ref[0].astype(f32) * EXPO)
    query = jnp.concatenate([hi, lo], axis=0)

    long = long_ref[0] == 1
    lo = jnp.where(long, 0, qb)
    hi = jnp.where(long, blocks, qb + 1)
    acc[...] = jnp.zeros_like(acc)

    def score(r, top):
        s = mm(kk[pl.ds(pl.multiple_of(r * rows, rows), rows), :], query, 1, 0)
        scores[r] = s
        return jnp.maximum(top, jnp.max(s, axis=0, keepdims=True))

    top = lax.fori_loop(lo, hi, score, jnp.full((1, rows), -1e30, f32))

    def weigh(r, total):
        e = jnp.exp2(scores[r] - top)
        acc[...] += mm(v_ref[r], e.astype(bf16), 1, 0)
        return total + jnp.sum(e, axis=0, keepdims=True)

    total = lax.fori_loop(lo, hi, weigh, jnp.zeros((1, rows), f32))
    out = acc[...] / total
    of_ref[0] = out
    o_ref[0] = out.astype(bf16)
    l_ref[0, 0] = top + jnp.log2(total)


def backward_kernel(
    long_ref, q_ref, k_ref, v_ref, do_ref, of_ref, l_ref, cos_ref, sin_ref,
    dq_ref, dk_ref, dv_ref, kk, vv, dk, dv, dq,
):
    blocks, _, rows = k_ref.shape
    qb = pl.program_id(1)

    @pl.when(qb == 0)
    def _():
        for r in range(blocks):
            k, v = k_ref[r], v_ref[r]
            one = jnp.ones((HEAD_DIM, rows), bf16)
            span = slice(r * rows, (r + 1) * rows)
            kk[span, :] = jnp.concatenate([k, k, one, one], axis=0).T
            vv[span, :] = jnp.concatenate([v, one], axis=0).T
        dk[...] = jnp.zeros_like(dk)
        dv[...] = jnp.zeros_like(dv)

    q = q_ref[0]
    do = do_ref[0]
    hi, lo = split_two(q.astype(f32) * EXPO)
    query = jnp.concatenate([hi, lo, three_rows(-l_ref[0, 0], 2 * HEAD_DIM)], axis=0)
    delta = jnp.sum(do.astype(f32) * of_ref[0], axis=0, keepdims=True)
    grad = jnp.concatenate([do, three_rows(-delta, HEAD_DIM)], axis=0)
    q_rows = q.T
    do_rows = do.T
    cos, sin = cos_ref[qb], sin_ref[qb]

    long = long_ref[0] == 1
    dq[...] = jnp.zeros_like(dq)

    def one(r, carry):
        span = pl.ds(pl.multiple_of(r * rows, rows), rows)
        p = jnp.exp2(mm(kk[span, :], query, 1, 0))
        ds = (p * mm(vv[span, :], grad, 1, 0)).astype(bf16)
        dv[span, :] += mm(p.astype(bf16), do_rows, 1, 0)
        dk[span, :] += mm(ds, q_rows, 1, 0)
        dq[...] += mm(k_ref[r], ds, 1, 0)
        return carry

    lax.fori_loop(jnp.where(long, 0, qb), jnp.where(long, blocks, qb + 1), one, 0)
    dq_ref[0] = rope_back(dq[...] * 0.125, cos, sin).astype(bf16)

    @pl.when(qb == blocks - 1)
    def _():
        for r in range(blocks):
            span = slice(r * rows, (r + 1) * rows)
            dk_ref[r] = rope_back(dk[span, :].T * 0.125, cos_ref[r], sin_ref[r]).astype(bf16)
            dv_ref[r] = dv[span, :].T.astype(bf16)


def grad_h_kernel(*refs):
    parts, w_ref, dh_ref = refs[:-2], refs[-2], refs[-1]
    g = jnp.concatenate([r[0] for r in parts], axis=0)
    dh_ref[0] = mm(g.T, w_ref[...], 1, 0).astype(bf16)


def grad_w_kernel(*refs):
    parts, h_ref, dw_ref, acc = refs[:-3], refs[-3], refs[-2], refs[-1]
    b = pl.program_id(0)
    g = jnp.concatenate([r[0] for r in parts], axis=0)
    dw = mm(g, h_ref[0], 1, 0)

    @pl.when(b == 0)
    def _():
        acc[...] = dw

    @pl.when(b > 0)
    def _():
        acc[...] += dw

    @pl.when(b == pl.num_programs(0) - 1)
    def _():
        dw_ref[...] = acc[...].astype(bf16)


def ffn_kernel(
    h_ref, g_ref, bd_ref, b_ref, w0, w1, w2, w3,
    mo_ref, dh_ref, db_ref, d0, d1, d2, d3, h_t, g_t, w_ref, dw_ref,
):
    i = pl.program_id(0)
    tiles = pl.num_programs(0) // 4

    @pl.when(i == 0)
    def _():
        h_t[...] = h_ref[...].T
        g_t[...] = g_ref[...].T
        mo_ref[...] = jnp.broadcast_to(bd_ref[...], mo_ref.shape)
        dh_ref[...] = jnp.zeros_like(dh_ref)

    for n, ref in enumerate((w0, w1, w2, w3)):

        @pl.when(i // tiles == n)
        def _(ref=ref):
            w_ref[...] = ref[...]

    rows = w_ref.shape[0]
    bias = jnp.broadcast_to(b_ref[...], (128, rows)).T[:, :1]
    up = mm(w_ref[:, :D], h_t[...], 1, 0) + bias
    root = math.sqrt(2.0 / math.pi)
    square = up * up
    t = jnp.tanh(root * up * (1.0 + 0.044715 * square))
    half_t = 0.5 + 0.5 * t
    act = (up * half_t).astype(bf16)
    slope = half_t + 0.5 * up * (1.0 - t * t) * (root * (1.0 + 3.0 * 0.044715 * square))
    dup = (mm(w_ref[:, D:], g_t[...], 1, 0) * slope).astype(bf16)
    dw_ref[:, :D] = mm(dup, h_ref[...], 1, 0).astype(bf16)
    dw_ref[:, D:] = mm(act, g_ref[...], 1, 0).astype(bf16)
    dup_t = dup.T
    mo_ref[...] += mm(act.T, w_ref[:, D:], 1, 0)
    dh_ref[...] += mm(dup_t, w_ref[:, :D], 1, 0)
    db_ref[...] = mm(jnp.ones((16, dup_t.shape[0]), bf16), dup_t, 1, 0)[:1]

    for n, ref in enumerate((d0, d1, d2, d3)):

        @pl.when(i // tiles == n)
        def _(ref=ref):
            ref[...] = dw_ref[...]


def full(shape):
    return pl.BlockSpec(shape, lambda *_: (0,) * len(shape))


SMEM = pl.BlockSpec(memory_space=pltpu.SMEM)
ONE = pltpu.CompilerParams(dimension_semantics=("arbitrary",))
TWO = pltpu.CompilerParams(dimension_semantics=("arbitrary", "arbitrary"))


def qkv_call(pa, pb, xs, gain, shift, was, wbs, cos, sin):
    blocks = len(xs)
    rows = xs[0].shape[1]
    seat_rows = 2 * was[0].shape[0] * 2 * was[0].shape[1]
    feats = 3 * seat_rows // 4
    block = lambda *s: pl.BlockSpec((1,) + s, lambda b: (b, 0, 0))
    return pl.pallas_call(
        qkv_kernel,
        name="qkv",
        grid=(blocks,),
        in_specs=[SMEM, SMEM]
        + [full((1, rows, D))] * blocks
        + [block(1, D), block(1, D)]
        + [full(was[0].shape)] * 4
        + [block(HALF, rows), block(HALF, rows)],
        out_specs=[block(rows, D), block(feats, rows), full((feats, D)), full((seat_rows - feats, D))],
        out_shape=[
            jax.ShapeDtypeStruct((blocks, rows, D), bf16),
            jax.ShapeDtypeStruct((blocks, feats, rows), bf16),
            jax.ShapeDtypeStruct((feats, D), bf16),
            jax.ShapeDtypeStruct((seat_rows - feats, D), bf16),
        ],
        scratch_shapes=[pltpu.VMEM((rows, D), f32)],
        compiler_params=ONE,
    )(pa, pb, *xs, gain, shift, *was, *wbs, cos, sin)


def forward_call(long, qkv, heads, head):
    blocks, _, rows = qkv.shape
    part = lambda n: pl.BlockSpec((blocks, HEAD_DIM, rows), lambda h, b, n=n: (0, n * heads + head, 0))
    own = pl.BlockSpec((1, HEAD_DIM, rows), lambda h, b: (b, head, 0))
    out = pl.BlockSpec((1, HEAD_DIM, rows), lambda h, b: (b, 0, 0))
    return pl.pallas_call(
        forward_kernel,
        name="attn_fwd",
        grid=(1, blocks),
        in_specs=[SMEM, own, part(1), part(2)],
        out_specs=[out, out, pl.BlockSpec((1, 1, 1, rows), lambda h, b: (0, b, 0, 0))],
        out_shape=[
            jax.ShapeDtypeStruct((blocks, HEAD_DIM, rows), bf16),
            jax.ShapeDtypeStruct((blocks, HEAD_DIM, rows), f32),
            jax.ShapeDtypeStruct((1, blocks, 1, rows), f32),
        ],
        scratch_shapes=[
            pltpu.VMEM((blocks * rows, 2 * HEAD_DIM), bf16),
            pltpu.VMEM((blocks, rows, rows), f32),
            pltpu.VMEM((HEAD_DIM, rows), f32),
        ],
        compiler_params=TWO,
    )(long, qkv, qkv, qkv)


def backward_call(long, qkv, do, of, lse, cos, sin, heads, head):
    blocks, _, rows = qkv.shape
    part = lambda n: pl.BlockSpec((blocks, HEAD_DIM, rows), lambda h, b, n=n: (0, n * heads + head, 0))
    own = pl.BlockSpec((1, HEAD_DIM, rows), lambda h, b: (b, head, 0))
    out = pl.BlockSpec((1, HEAD_DIM, rows), lambda h, b: (b, 0, 0))
    whole = pl.BlockSpec((blocks, HEAD_DIM, rows), lambda h, b: (0, 0, 0))
    shape = jax.ShapeDtypeStruct((blocks, HEAD_DIM, rows), bf16)
    return pl.pallas_call(
        backward_kernel,
        name="attn_bwd",
        grid=(1, blocks),
        in_specs=[SMEM, own, part(1), part(2), own, out, pl.BlockSpec((1, 1, 1, rows), lambda h, b: (0, b, 0, 0)), full(cos.shape), full(sin.shape)],
        out_specs=[out, whole, whole],
        out_shape=[shape, shape, shape],
        scratch_shapes=[
            pltpu.VMEM((blocks * rows, 4 * HEAD_DIM), bf16),
            pltpu.VMEM((blocks * rows, 2 * HEAD_DIM), bf16),
            pltpu.VMEM((blocks * rows, HEAD_DIM), f32),
            pltpu.VMEM((blocks * rows, HEAD_DIM), f32),
            pltpu.VMEM((HEAD_DIM, rows), f32),
        ],
        compiler_params=TWO,
    )(long, qkv, qkv, qkv, do, of, lse, cos, sin)


def grad_h_call(parts, w):
    blocks, feats, rows = parts[0].shape
    back = lambda *s: pl.BlockSpec((1,) + s, lambda b: (blocks - 1 - b, 0, 0))
    return pl.pallas_call(
        grad_h_kernel,
        name="grad_h",
        grid=(blocks,),
        in_specs=[back(feats, rows)] * len(parts) + [full(w.shape)],
        out_specs=back(rows, D),
        out_shape=jax.ShapeDtypeStruct((blocks, rows, D), bf16),
        compiler_params=ONE,
    )(*parts, w)


def grad_w_call(parts, h):
    blocks, feats, rows = parts[0].shape
    block = lambda *s: pl.BlockSpec((1,) + s, lambda b: (b, 0, 0))
    shape = (feats * len(parts), D)
    return pl.pallas_call(
        grad_w_kernel,
        name="grad_w",
        grid=(blocks,),
        in_specs=[block(feats, rows)] * len(parts) + [block(rows, D)],
        out_specs=full(shape),
        out_shape=jax.ShapeDtypeStruct(shape, bf16),
        scratch_shapes=[pltpu.VMEM(shape, f32)],
        compiler_params=ONE,
    )(*parts, h)


def ffn_call(h, g, bias_down, bias, weights):
    rows = h.shape[0]
    hidden = weights[0].shape[0]
    tiles = 2
    tile = hidden // tiles
    wide = [
        pl.BlockSpec((tile, 2 * D), lambda i, n=n: (jnp.clip(i - n * tiles, 0, tiles - 1), 0))
        for n in range(4)
    ]
    flat = pl.BlockSpec((1, tile), lambda i: (0, i))
    token = full((rows, D))
    return pl.pallas_call(
        ffn_kernel,
        name="ffn",
        grid=(4 * tiles,),
        in_specs=[token, token, full((1, D)), flat] + wide,
        out_specs=[token, token, flat] + wide,
        out_shape=[
            jax.ShapeDtypeStruct((rows, D), f32),
            jax.ShapeDtypeStruct((rows, D), f32),
            jax.ShapeDtypeStruct((1, 4 * hidden), f32),
        ]
        + [jax.ShapeDtypeStruct((hidden, 2 * D), bf16)] * 4,
        scratch_shapes=[
            pltpu.VMEM((D, rows), bf16),
            pltpu.VMEM((D, rows), bf16),
            pltpu.VMEM((tile, 2 * D), bf16),
            pltpu.VMEM((tile, 2 * D), bf16),
        ],
        compiler_params=ONE,
    )(h, g, bias_down, bias, *weights)


def on_device(
    tokens, cotangent, cond, seq_lengths,
    adaptive_master, attention_master, feedforward_master, vector_master,
    adaptive_first, attention_first, feedforward_first, vector_first,
    adaptive_second, attention_second, feedforward_second, vector_second,
):
    rows = tokens.shape[0]
    seq_size = lax.axis_size("seq")
    batch_size = lax.axis_size("batch")
    world = seq_size * batch_size
    heads = HEADS // seq_size
    seat = lax.axis_index("seq")
    place = lax.axis_index("batch")
    me = place * seq_size + seat
    seq_stages = [("seq", b) for b in bits_down(seq_size)]
    batch_bits = bits_down(batch_size)
    far_first = [("batch", b) for b in batch_bits]
    near_first = [("batch", batch_bits[-1])] + [("batch", b) for b in batch_bits[:-1]]
    seq_masks = masks_of(seq_stages, seq_size)
    chunk = attention_master.shape[1]
    half = chunk // 2

    cs = jax.nn.silu(cond.astype(f32)).astype(bf16)
    split = (seq_lengths[1] > 0).astype(jnp.int32)
    vec_part = vector_master.shape[0]
    vec_rows = -(-vec_part // COND)
    vec_pad = jnp.pad(vector_master.astype(bf16), (0, vec_rows * COND - vec_part))
    flag = jnp.full((1, COND), 1.0, bf16) * split.astype(bf16)
    small = jnp.concatenate([cs, flag, vec_pad.reshape(vec_rows, COND)], axis=0)
    small = jnp.broadcast_to(small[None], (world,) + small.shape)
    small_all = lax.all_to_all(small, ALL, 0, 0, tiled=True)
    cs_all = small_all[::seq_size, :SLOTS].reshape(batch_size * SLOTS, COND)
    split_all = small_all[::seq_size, SLOTS, 0] > 0
    vector_f = small_all[:, SLOTS + 1 :].reshape(world, vec_rows * COND)[:, :vec_part]
    vector_f = vector_f.reshape(-1).astype(f32)
    gain_one = vector_f[:D]
    gain_two = vector_f[D : 2 * D]
    bias_mod = vector_f[3 * D + FF :]
    mod_part = adaptive_master.shape[1]
    mod_cols = mm(cs_all, adaptive_master.astype(bf16), 1, 0)
    mod_send = jnp.broadcast_to(
        mod_cols.reshape(batch_size, 1, SLOTS, mod_part), (batch_size, seq_size, SLOTS, mod_part)
    ).reshape(world, SLOTS, mod_part)
    mod_got = lax.all_to_all(mod_send, ALL, 0, 0, tiled=True)
    mod = jnp.swapaxes(mod_got, 0, 1).reshape(SLOTS, world * mod_part) + bias_mod

    own = tokens[None]
    y_first, core_last = seq_stages
    x_y = swap(own, y_first)
    x_c = swap(own, core_last)
    x_yc = swap(x_y, core_last)
    slot_of = [split * (seat ^ m) for m in seq_masks]
    mod_here = [lax.dynamic_index_in_dim(mod, s, 0, keepdims=True) for s in slot_of]
    gain_rows = jnp.stack([gain_one * (1.0 + m[:, D : 2 * D]) for m in mod_here])
    shift_rows = jnp.stack([m[:, :D] for m in mod_here])
    own_mod = mod_here[0]
    scale_one = own_mod[:, D : 2 * D]
    gate_one = own_mod[:, 2 * D : 3 * D]
    shift_two = own_mod[:, 3 * D : 4 * D]
    scale_two = own_mod[:, 4 * D : 5 * D]
    gate_two = own_mod[:, 5 * D :]
    freqs = 10000.0 ** (-jnp.arange(HALF, dtype=f32) * 2.0 / HEAD_DIM)
    starts = jnp.stack([(1 - split) * (seat ^ m) * rows for m in seq_masks])
    pos = (starts[:, None] + jnp.arange(rows, dtype=jnp.int32)[None]).astype(f32)
    angles = pos[:, None, :] * freqs[None, :, None]
    cos, sin = jnp.cos(angles), jnp.sin(angles)
    long = (1 - split).reshape(1)

    kinds = 4
    per_seat = batch_size // kinds
    moves = []
    for j in range(world):
        kind, r = divmod(j, world // kinds)
        s, low = divmod(r, per_seat)
        moves.append((j, (kind * per_seat + low) * seq_size + s))
    att_piece = lax.ppermute(attention_master.T.astype(bf16), ALL, moves)
    att_a = gather_rel(att_piece[None, :half], far_first[:-1])
    att_b = gather_rel(att_piece[None, half:], near_first[:-1])
    att_a = (att_a, swap(att_a, far_first[-1]))
    att_b = (att_b, swap(att_b, near_first[-1]))
    order = jnp.arange(batch_size, dtype=jnp.int32) ^ place
    pa, pb = place_of(order, far_first, 1), place_of(order, near_first, 1)
    h1_all, qkv, qkv_w, wo_own = qkv_call(
        pa, pb, (own, x_y, x_c, x_yc), gain_rows, shift_rows, att_a, att_b, cos, sin
    )

    wo_rel = gather_rel(wo_own[None], seq_stages)
    to_abs = lambda parts: flip(jnp.stack([parts[k] for k in places_of(seq_stages, seq_size, seq_size)]), seat)
    to_rel = lambda v: [flip(v, seat)[m] for m in seq_masks]
    wo_t = to_abs(wo_rel).reshape(D, D)

    up_t = feedforward_master[0].T.astype(bf16)
    down_t = feedforward_master[1].T.astype(bf16)
    both = jnp.concatenate([up_t, down_t], axis=1)
    y_stage, core_stage = seq_stages[:-1], seq_stages[-1:]
    stages_a = far_first + y_stage + core_stage
    stages_b = y_stage + far_first + core_stage
    ff_a = gather_rel(both[None, :half], stages_a[:-1])
    ff_b = gather_rel(both[None, half:], stages_b[:-1])
    wide = lambda v: v.reshape(-1, 2 * D)
    ff_a2 = wide(swap(ff_a, core_stage[0]))
    ff_b2 = wide(swap(ff_b, core_stage[0]))
    ff_a, ff_b = wide(ff_a), wide(ff_b)
    masks_a = jnp.array(masks_of(stages_a, seq_size), jnp.int32)
    masks_b = jnp.array(masks_of(stages_b, seq_size), jnp.int32)

    def spread(parts):
        return [parts[0]] + [swap(parts[k], ("seq", seq_masks[k])) for k in range(1, seq_size)]

    kept = []
    o_heads = []
    for n in range(heads):
        o_n, o_f, lse = forward_call(long, qkv, heads, n)
        kept.append((o_f, lse))
        if n == 0:
            vector_f, _ = lax.optimization_barrier((vector_f, lse))
            bias_up_rows = vector_f[2 * D : 2 * D + FF].reshape(world, chunk)
            bias_down = vector_f[2 * D + FF : 3 * D + FF]
            bias_a = one_hot_pick(masks_a ^ me, bias_up_rows[:, :half])
            bias_b = one_hot_pick(masks_b ^ me, bias_up_rows[:, half:])
            bias_hidden = jnp.concatenate([bias_a, bias_b]).reshape(1, FF)
        o_heads.append(spread(o_n))
    o_parts = [jnp.concatenate([h[k] for h in o_heads], axis=0) for k in range(seq_size)]
    o_t = to_abs(o_parts).reshape(D, rows)
    attn_out = mm(o_t, wo_t, 0, 1)
    inputs_f = tokens.astype(f32)
    middle = inputs_f + gate_one * attn_out

    centre = middle - jnp.mean(middle, axis=-1, keepdims=True)
    rstd_two = lax.rsqrt(jnp.mean(centre * centre, axis=-1, keepdims=True) + norm_eps)
    n_two = centre * rstd_two
    gain_two_all = gain_two * (1.0 + scale_two)
    h2 = (n_two * gain_two_all + shift_two).astype(bf16)
    grad_out = cotangent.astype(f32)
    gm = (grad_out * gate_two).astype(bf16)
    ffn_out, grad_h2, db, da, da2, dbb, dbb2 = ffn_call(
        h2, gm, bias_down[None], bias_hidden, (ff_a, ff_a2, ff_b, ff_b2)
    )
    block_output = (middle + gate_two * ffn_out).astype(bf16)
    grad_bias_down = jnp.sum(gm.astype(f32), axis=0)
    dgt2 = jnp.sum(grad_out * ffn_out, axis=0)
    dsh2 = jnp.sum(grad_h2, axis=0)
    hn2 = jnp.sum(grad_h2 * n_two, axis=0)
    dsc2 = hn2 * gain_two
    dg2 = hn2 * (1.0 + scale_two[0])
    dn = grad_h2 * gain_two_all
    grad_middle = grad_out + rstd_two * (
        dn
        - jnp.mean(dn, axis=-1, keepdims=True)
        - n_two * jnp.mean(dn * n_two, axis=-1, keepdims=True)
    )
    dgt1 = jnp.sum(grad_middle * attn_out, axis=0)
    ga = (grad_middle * gate_one).astype(bf16)
    do_t = mm(wo_t, ga, 0, 1).astype(bf16).reshape(seq_size, heads * HEAD_DIM, rows)
    do_all = jnp.stack(spread(to_rel(do_t)))
    d_wo = mm(ga, o_t, 0, 1).astype(bf16).reshape(seq_size, D // seq_size, D)
    pieces = lambda v: v.reshape(world // 2, half, 2 * D)
    ff_sum_a = scatter_two(pieces(da), pieces(da2), stages_a)[0]
    ff_sum_b = scatter_two(pieces(dbb), pieces(dbb2), stages_b)[0]
    wo_sum = scatter_rel(jnp.stack(to_rel(d_wo)), seq_stages)[0]

    head_grads = []
    for n in range(heads):
        head_grads.append(backward_call(long, qkv, do_all, *kept[n], cos, sin, heads, n))
    parts = [g[k] for k in range(3) for g in head_grads]
    grad_h1_all = grad_h_call(parts, qkv_w)
    d_qkv_w = grad_w_call(parts, h1_all)
    att_grad = jnp.concatenate([d_qkv_w, wo_sum], axis=0).reshape(batch_size, chunk, D)
    att_grad = flip(att_grad, place)
    ordered = lambda v, stages: jnp.stack([v[m] for m in masks_of(stages, 1)])
    att_sum = jnp.concatenate(
        [
            scatter_rel(ordered(att_grad[:, :half], far_first), far_first)[0],
            scatter_rel(ordered(att_grad[:, half:], near_first), near_first)[0],
        ],
        axis=0,
    )
    att_sum = lax.ppermute(att_sum, ALL, [(b, a) for a, b in moves])

    grad_h1 = scatter_rel(grad_h1_all, seq_stages)[0].astype(f32)
    centre = inputs_f - jnp.mean(inputs_f, axis=-1, keepdims=True)
    rstd_one = lax.rsqrt(jnp.mean(centre * centre, axis=-1, keepdims=True) + norm_eps)
    n_one = centre * rstd_one
    dsh1 = jnp.sum(grad_h1, axis=0)
    hn1 = jnp.sum(grad_h1 * n_one, axis=0)
    dsc1 = hn1 * gain_one
    dg1 = hn1 * (1.0 + scale_one[0])
    dn = grad_h1 * (gain_one * (1.0 + scale_one))
    input_grad = grad_middle + rstd_one * (
        dn
        - jnp.mean(dn, axis=-1, keepdims=True)
        - n_one * jnp.mean(dn * n_one, axis=-1, keepdims=True)
    )
    input_grad = input_grad.astype(bf16)

    dmod = jnp.concatenate([dsh1, dsc1, dgt1, dsh2, dsc2, dgt2])
    devices = jnp.arange(world, dtype=jnp.int32) ^ me
    exact = lax.Precision.HIGHEST
    bias_grad = jnp.concatenate(
        [
            one_hot_pick(
                place_of(devices, stages, seq_size),
                d,
                exact,
            )
            for d, stages in zip(db.reshape(2, world, half), (stages_a, stages_b))
        ],
        axis=1,
    ).reshape(-1)
    vec_grad = jnp.concatenate([dg1, dg2, bias_grad, grad_bias_down, dmod])
    tail = jnp.concatenate(
        [dmod.reshape(world, mod_part), vec_grad.reshape(world, vec_part)], axis=1
    )
    tail_all = lax.all_to_all(tail[:, None], ALL, 0, 0, tiled=True)[:, 0]
    vector_sum = jnp.sum(tail_all[:, mod_part:], axis=0)
    slots = jnp.arange(seq_size, dtype=jnp.int32)[None, :] * split_all[:, None].astype(jnp.int32)
    rows_of = (jnp.arange(batch_size, dtype=jnp.int32)[:, None] * SLOTS + slots).reshape(-1)
    cs_dev = one_hot_pick(rows_of, cs_all.astype(f32))
    adaptive_sum = lax.dot_general(
        cs_dev, tail_all[:, :mod_part], (((0,), (0,)), ((), ())), precision=lax.Precision.HIGHEST
    )

    attention_sum = att_sum.astype(f32).T
    ff_sum = jnp.concatenate([ff_sum_a, ff_sum_b], axis=0).astype(f32)
    forward_sum = jnp.stack([ff_sum[:, :D].T, ff_sum[:, D:].T])
    adaptive_res = adamw_update(
        adaptive_master, adaptive_first, adaptive_second, adaptive_sum, rate_adaptive
    )
    attention_res = adamw_update(
        attention_master, attention_first, attention_second, attention_sum, rate_attention
    )
    forward_res = adamw_update(
        feedforward_master, feedforward_first, feedforward_second, forward_sum, rate_forward
    )
    vector_res = adamw_update(vector_master, vector_first, vector_second, vector_sum, rate_vector)
    return (block_output, input_grad, *adaptive_res, *attention_res, *forward_res, *vector_res)


def solution(mesh):
    rows = P(ALL, None)
    cols = P(None, ALL)
    deep = P(None, None, ALL)
    flat = P(ALL)
    return jax.shard_map(
        on_device,
        mesh=mesh,
        in_specs=(rows, rows, P("batch", None), P("batch")) + (cols, cols, deep, flat) * 3,
        out_specs=(rows, rows) + (cols,) * 8 + (deep,) * 4 + (flat,) * 4,
        check_vma=False,
    )
```
